32 devices in a mesh: scene: 2 (over y), tok: 8 (over z, x), hid: 2 (over core).
Axes of the slice: x: 2, y: 2, z: 4, core: 2. Of those that a mesh axis runs over, the one named last changes fastest.
Arguments:
- input_keys: bfloat16 [16384, 384], P(('scene', 'tok'), 'hid'), parts along dimension 0, may hold values from -6 to 6
- input_values: bfloat16 [16384, 384], P(('scene', 'tok'), 'hid'), parts along dimension 0, may hold values from -6 to 6
- input_lr: float32 [16384], P(('scene', 'tok')), parts along dimension 0, may hold values from 0.1 to 1
- gate_weight: bfloat16 [384, 1536], P('tok', 'hid'), may hold values from -0.3125 to 0.3125
- up_weight: bfloat16 [384, 1536], P('tok', 'hid'), may hold values from -0.3125 to 0.3125
- down_weight: bfloat16 [384, 1536], P('tok', 'hid'), may hold values from -0.15625 to 0.15625
- queries: bfloat16 [2048, 384], P(('scene', 'tok'), 'hid'), parts along dimension 0, may hold values from -6 to 6
- out_grad: bfloat16 [2048, 384], P(('scene', 'tok'), 'hid'), parts along dimension 0, may hold values from -6 to 6
Outputs:
- target_out: bfloat16 [2048, 384], P(('scene', 'tok'), 'hid'), parts along dimension 0
- query_grad: bfloat16 [2048, 384], P(('scene', 'tok'), 'hid'), parts along dimension 0
The draws below stay inside these ranges and needn't reach their ends.
There are 2 independent parts, one for each index of `scene`. The reference program is written for one: setup_inputs(seed, part) draws one part's arguments, and reference() takes and returns one part's arrays. A program takes and returns all parts, laid end to end along the dimension named above; an argument that names none is the same for every part. Nothing has to cross between parts.
All inputs are finite; a program needn't handle non-finite values.
Results may differ from the reference program's by a relative error of at most 0.009.
Values may be sent and summed in bfloat16 or wider, within the bound.
A program may use at most 64 MiB of HBM per device.

```python
import math
import jax
import jax.numpy as jnp
from jax import lax

D = 384
HID = 1536
TIN = 8192
TTG = 1024


def raised(drawn, stream_key, source, target, blocks, factor):
    def block_of(position):
        return (jnp.arange(drawn.shape[position]) // (drawn.shape[position] // blocks)).reshape((-1,) + (1,) * (drawn.ndim - 1 - position))

    near = jax.random.permutation(stream_key, blocks)[block_of(target)]
    far = (block_of(target) + blocks // 2) % blocks
    return jnp.where((block_of(source) == near) | (block_of(source) == far), factor * drawn, drawn)


def block_levels(own_key, shape, shards, low, high):
    def one(position, blocks):
        heights = jax.random.uniform(jax.random.fold_in(jax.random.fold_in(own_key, 6), position), (blocks,), jnp.float32, low / len(shards), high / len(shards))
        return jnp.repeat(jnp.exp(heights), shape[position] // blocks).reshape((-1,) + (1,) * (len(shape) - position - 1))

    loudness = one(*shards[0])
    for cut in shards[1:]:
        loudness = loudness * one(*cut)
    return loudness


def noise(rng, dims, scale, limit, cuts=(), held_as=jnp.bfloat16):
    drawn = scale * jax.random.normal(rng, dims, jnp.float32)
    if cuts:
        drawn = drawn * block_levels(rng, dims, cuts, -0.22, 0.18)
    return jnp.clip(drawn, -limit, limit).astype(held_as)


def bell_draw_with(own_key, extent, spread, reach, pieces, heavy, held_as=jnp.bfloat16):
    result = spread * jax.random.normal(own_key, extent, jnp.float32)
    if pieces:
        result = result * block_levels(own_key, extent, pieces, -0.22, 0.18)
    return jnp.clip(raised(result, jax.random.fold_in(own_key, 3), *heavy), -reach, reach).astype(held_as)


def setup_inputs(seed: int = 0, part: int = 0) -> dict:
    splits = jax.random.split(jax.random.key(seed), 9)
    part_keys = jax.random.split(jax.random.fold_in(splits[8], part), 9)
    return {
        "input_keys": bell_draw_with(part_keys[0], (TIN, D), 1.0, 6.0, ((0, 8), (1, 2)), (0, 1, 8, 2.0)),
        "input_values": bell_draw_with(part_keys[1], (TIN, D), 1.0, 6.0, ((0, 8), (1, 2)), (0, 1, 8, 2.0)),
        "input_lr": jnp.clip(jnp.exp(math.log(1.0) - 2.3025851 * jax.random.uniform(part_keys[2], (TIN,), jnp.float32) ** block_levels(part_keys[2], (TIN,), ((0, 8),), -0.2, 0.2)), 0.1, 1.0),
        "gate_weight": noise(splits[3], (D, HID), D ** -0.5, 0.3125, ((0, 8), (1, 2))),
        "up_weight": noise(splits[4], (D, HID), D ** -0.5, 0.3125, ((0, 8), (1, 2))),
        "down_weight": noise(splits[5], (D, HID), HID ** -0.5, 0.15625, ((0, 8), (1, 2))),
        "queries": noise(part_keys[6], (TTG, D), 1.0, 6.0, ((0, 8), (1, 2))),
        "out_grad": noise(part_keys[7], (TTG, D), 1.0, 6.0, ((0, 8), (1, 2))),
    }


step_ratio = 0.5
epsilon = 1e-06

def silu_slope(pre):
    sigma = jax.nn.sigmoid(pre)
    return sigma * (1.0 + pre * (1.0 - sigma))

def contract_rows(left, right):
    return lax.dot_general(left, right, (((0,), (0,)), ((), ())), preferred_element_type=jnp.float32)

def contract_cols(left, right):
    return lax.dot_general(left, right, (((1,), (1,)), ((), ())), preferred_element_type=jnp.float32)

def renew(weight, grad):
    base = weight.astype(jnp.float32)
    wsq = lax.optimization_barrier(jnp.sum(base * base, axis=1)) / HID
    gsq = lax.optimization_barrier(jnp.sum(grad * grad, axis=1)) / HID
    scale = step_ratio * jnp.sqrt(wsq) / jnp.sqrt(gsq + epsilon)
    moved = base - scale[:, None] * grad
    msq = lax.optimization_barrier(jnp.sum(moved * moved, axis=1)) / HID
    return (moved * (jnp.sqrt(wsq) / jnp.sqrt(msq + epsilon))[:, None]).astype(jnp.bfloat16)

def reference(input_keys, input_values, input_lr, gate_weight, up_weight, down_weight, queries, out_grad):
    total_in = input_keys.shape[0]
    block_in = min(total_in, 4096)
    count_in = total_in // block_in
    key_blocks = input_keys.reshape(count_in, block_in, D)
    value_blocks = input_values.reshape(count_in, block_in, D)
    rate_blocks = input_lr.reshape(count_in, block_in)

    def accumulate(carry, item):
        keys, values, rates = item
        scaled = (rates[:, None] * values.astype(jnp.float32)).astype(jnp.bfloat16)
        key_gate = jnp.dot(keys, gate_weight, preferred_element_type=jnp.float32)
        key_up = jnp.dot(keys, up_weight, preferred_element_type=jnp.float32)
        gate_act = jax.nn.silu(key_gate)
        key_act = (gate_act * key_up).astype(jnp.bfloat16)
        back = jnp.dot(scaled, down_weight, preferred_element_type=jnp.float32)
        d_gate = (-back * key_up * silu_slope(key_gate)).astype(jnp.bfloat16)
        d_up = (-back * gate_act).astype(jnp.bfloat16)
        grad_gate = carry[0] + contract_rows(keys, d_gate)
        grad_up = carry[1] + contract_rows(keys, d_up)
        grad_down = carry[2] - contract_rows(scaled, key_act)
        return ((grad_gate, grad_up, grad_down), None)
    zeros = jnp.zeros((D, HID), jnp.float32)
    (grad_gate, grad_up, grad_down), _ = lax.scan(accumulate, (zeros, zeros, zeros), (key_blocks, value_blocks, rate_blocks))
    new_gate = renew(gate_weight, grad_gate)
    new_up = renew(up_weight, grad_up)
    new_down = renew(down_weight, grad_down)
    total_tg = queries.shape[0]
    block_tg = min(total_tg, 4096)
    count_tg = total_tg // block_tg

    def apply_block(item):
        query_rows, grad_rows = item
        query_gate = jnp.dot(query_rows, new_gate, preferred_element_type=jnp.float32)
        query_up = jnp.dot(query_rows, new_up, preferred_element_type=jnp.float32)
        gate_act = jax.nn.silu(query_gate)
        query_act = (gate_act * query_up).astype(jnp.bfloat16)
        target_out = contract_cols(query_act, new_down).astype(jnp.bfloat16)
        query_back = jnp.dot(grad_rows, new_down, preferred_element_type=jnp.float32)
        q_gate_grad = (query_back * query_up * silu_slope(query_gate)).astype(jnp.bfloat16)
        q_up_grad = (query_back * gate_act).astype(jnp.bfloat16)
        query_grad = (contract_cols(q_gate_grad, new_gate) + contract_cols(q_up_grad, new_up)).astype(jnp.bfloat16)
        return (target_out, query_grad)
    outs_blocks, grad_blocks = lax.map(apply_block, (queries.reshape(count_tg, block_tg, D), out_grad.reshape(count_tg, block_tg, D)))
    return (outs_blocks.reshape(total_tg, D), grad_blocks.reshape(total_tg, D))
```

```python
import functools

import jax
import jax.numpy as jnp
from jax import lax
from jax.experimental import pallas as pl
from jax.experimental.pallas import tpu as pltpu
from jax.sharding import PartitionSpec as P

HID = 1536


step_ratio = 0.5
epsilon = 1e-06


def silu_slope(pre):
    sigma = jax.nn.sigmoid(pre)
    return sigma * (1.0 + pre * (1.0 - sigma))


def contract_rows(left, right):
    return lax.dot_general(
        left, right, (((0,), (0,)), ((), ())), preferred_element_type=jnp.float32
    )


def contract_cols(left, right):
    return lax.dot_general(
        left, right, (((1,), (1,)), ((), ())), preferred_element_type=jnp.float32
    )


def finish(moved, wsq, msq):
    return (moved * (jnp.sqrt(wsq) / jnp.sqrt(msq + epsilon))[:, None]).astype(jnp.bfloat16)


def shards_plain(
    input_keys, input_values, input_lr, gate_weight, up_weight, down_weight, queries, out_grad
):
    keys, values = (
        lax.all_gather(input_keys, "hid", axis=1, tiled=True),
        lax.all_gather(input_values, "hid", axis=1, tiled=True),
    )
    w_gate, w_up, w_down = (
        lax.all_gather(gate_weight, "tok", axis=0, tiled=True),
        lax.all_gather(up_weight, "tok", axis=0, tiled=True),
        lax.all_gather(down_weight, "tok", axis=0, tiled=True),
    )
    scaled = (input_lr[:, None] * values.astype(jnp.float32)).astype(jnp.bfloat16)
    key_gate = jnp.dot(keys, w_gate, preferred_element_type=jnp.float32)
    key_up = jnp.dot(keys, w_up, preferred_element_type=jnp.float32)
    gate_act = jax.nn.silu(key_gate)
    key_act = (gate_act * key_up).astype(jnp.bfloat16)
    back = jnp.dot(scaled, w_down, preferred_element_type=jnp.float32)
    d_gate = (-back * key_up * silu_slope(key_gate)).astype(jnp.bfloat16)
    d_up = (-back * gate_act).astype(jnp.bfloat16)
    width = gate_weight.shape[1]
    grads = lax.psum(
        jnp.concatenate(
            [
                contract_rows(keys, d_gate),
                contract_rows(keys, d_up),
                -contract_rows(scaled, key_act),
            ],
            axis=1,
        ),
        "tok",
    )
    olds = (w_gate, w_up, w_down)
    pieces = [grads[:, :width], grads[:, width : 2 * width], grads[:, 2 * width :]]
    weights = [old.astype(jnp.float32) for old in olds]
    renewed = []
    stats = []
    for weight, grad in zip(weights, pieces):
        stats.append(jnp.sum(weight * weight, axis=1))
        stats.append(jnp.sum(weight * grad, axis=1))
        stats.append(jnp.sum(grad * grad, axis=1))
    totals = lax.psum(
        (stats[0], stats[1], stats[2], stats[3], stats[4], stats[5], stats[6], stats[7], stats[8]),
        "hid",
    )
    for index in range(3):
        wsq = totals[3 * index] / HID
        cross = totals[3 * index + 1] / HID
        gsq = totals[3 * index + 2] / HID
        scale = step_ratio * jnp.sqrt(wsq) / jnp.sqrt(gsq + epsilon)
        moved = weights[index] - scale[:, None] * pieces[index]
        msq = wsq - 2.0 * scale * cross + scale * scale * gsq
        renewed.append(finish(moved, wsq, msq))
    new_gate, new_up, new_down = (renewed[0], renewed[1], renewed[2])
    query_rows, grad_rows = (
        lax.all_gather(queries, "hid", axis=1, tiled=True),
        lax.all_gather(out_grad, "hid", axis=1, tiled=True),
    )
    query_gate = jnp.dot(query_rows, new_gate, preferred_element_type=jnp.float32)
    query_up = jnp.dot(query_rows, new_up, preferred_element_type=jnp.float32)
    query_silu = jax.nn.silu(query_gate)
    query_act = (query_silu * query_up).astype(jnp.bfloat16)
    out_part = contract_cols(query_act, new_down)
    query_back = jnp.dot(grad_rows, new_down, preferred_element_type=jnp.float32)
    q_gate_grad = (query_back * query_up * silu_slope(query_gate)).astype(jnp.bfloat16)
    q_up_grad = (query_back * query_silu).astype(jnp.bfloat16)
    grad_part = contract_cols(q_gate_grad, new_gate) + contract_cols(q_up_grad, new_up)
    out_sum, grad_sum = (
        lax.psum_scatter(
            out_part.astype(jnp.bfloat16), "hid", scatter_dimension=1, tiled=True
        ).astype(jnp.float32),
        lax.psum_scatter(
            grad_part.astype(jnp.bfloat16), "hid", scatter_dimension=1, tiled=True
        ).astype(jnp.float32),
    )
    return (out_sum.astype(jnp.bfloat16), grad_sum.astype(jnp.bfloat16))


MESH = pl.DeviceIdType.MESH
WIDE = 2
DEPTH = 4
HBM = pl.BlockSpec(memory_space=pltpu.HBM)
VM = pl.BlockSpec(memory_space=pltpu.VMEM)


def remote(src, dst, send, recv, **where):
    return pltpu.make_async_remote_copy(
        src_ref=src, dst_ref=dst, send_sem=send, recv_sem=recv,
        device_id=where, device_id_type=MESH,
    )


def whole_kernel(
    tok, hidden, pieces,
    keys_in, vals_in, lr, q_in, g_in, gate_in, up_in, down_in,
    result,
    toks, vraw, own, olds, turned, d_pre, acts, acc, mine, from_end, from_mid, total,
    stats, news, q, parts, got,
    local, old_send, old_recv, over_send, over_recv,
    tok_send, tok_recv, pass_send, pass_recv, ask_send, ask_recv,
    end_send, end_recv, mid_send, mid_recv, fin_send, fin_recv,
    stat_send, stat_recv, part_send, part_recv,
):
    f32, bf16 = jnp.float32, jnp.bfloat16
    scene, core, rank = lax.axis_index("scene"), lax.axis_index("hid"), lax.axis_index("tok")
    z, x = lax.div(rank, WIDE), lax.rem(rank, WIDE)
    color = lax.rem(z + x, 2)
    rows = gate_in.shape[0]
    half, tokens = keys_in.shape
    count = q_in.shape[1]
    width = olds.shape[2]
    wide = 2 * half
    near = z + 1 - 2 * lax.rem(z, 2)
    side = z * WIDE + 1 - x
    stack = near * WIDE + x
    is_end = (z == 0) | (z == DEPTH - 1)

    def same(level):
        return level * WIDE + lax.rem(color + level, 2)

    others = [lax.rem(rank + step, tok) for step in range(1, tok)]
    barrier = pltpu.get_barrier_semaphore()
    peers = [{"hid": 1 - core}, {"scene": 1 - scene}, {"tok": side, "hid": 1 - core}]
    peers += [{"tok": other} for other in others]
    for where in peers:
        pl.semaphore_signal(barrier, inc=1, device_id=where, device_id_type=MESH)

    loads = []
    for index, (src, dst) in enumerate((
        (vals_in, vraw),
        (keys_in, toks.at[0, core, :, 0:tokens]),
        (gate_in, own.at[0:rows]),
        (up_in, own.at[rows:2 * rows]),
        (down_in, own.at[2 * rows:3 * rows]),
        (q_in, q.at[0, core, :, 0:count]),
        (g_in, q.at[1, core, :, 0:count]),
    )):
        loads.append(pltpu.make_async_copy(src, dst, local.at[index]))
        loads[-1].start()
    loads[0].wait()
    toks[1, core, :, 0:tokens] = (lr[...] * vraw[...].astype(f32)).astype(bf16)
    for load in loads[1:]:
        load.wait()
    pl.semaphore_wait(barrier, len(peers))

    sends = []

    def go(copy):
        copy.start()
        sends.append(copy)

    swap = remote(toks.at[:, core, :, 0:tokens], toks.at[:, core, :, 0:tokens],
                  pass_send.at[0], pass_recv.at[0], hid=1 - core)
    go(swap)

    cuts = ((0, 64), (64, 3 * rows))
    for part, (low, high) in enumerate(cuts):
        @pl.when(scene == part)
        def _():
            for index, other in enumerate(others):
                shade = lax.rem(lax.div(other, WIDE) + lax.rem(other, WIDE), 2)
                at = pl.ds(pl.multiple_of(shade * width, width), width)
                remote(own.at[low:high, at], olds.at[rank, low:high], old_send.at[index],
                       old_recv.at[tok - 2 - index], tok=other).start()

    chunk = tokens // 4
    inward = []
    for index in range(4):
        at = pl.ds(index * chunk, chunk)
        to = pl.ds(tokens + index * chunk, chunk)
        where = side if index < 2 else stack
        copy = remote(toks.at[:, core, :, at], toks.at[:, core, :, to],
                      tok_send.at[index], tok_recv.at[index], tok=where)
        inward.append(copy)
    for index in (0, 2, 1, 3):
        go(inward[index])
    ask = remote(q.at[:, core, :, 0:count], q.at[:, core, :, count:2 * count],
                 ask_send.at[0], ask_recv.at[0], tok=side)
    go(ask)
    mycols = pl.ds(pl.multiple_of(color * width, width), width)
    olds[rank] = own[:, mycols]

    for part, (low, high) in enumerate(cuts):
        @pl.when(scene == part)
        def _():
            for index, other in enumerate(others):
                source = lax.rem(rank + index + 1, tok)
                block = olds.at[source, low:high]
                remote(block, block, old_send.at[index], old_recv.at[index], tok=other).wait_recv()
                remote(block, block, over_send.at[index], over_recv.at[index], scene=1 - scene).start()
    for part, (low, high) in enumerate(cuts):
        @pl.when(scene != part)
        def _():
            for index in range(tok - 1):
                source = lax.rem(rank + index + 1, tok)
                block = olds.at[source, low:high]
                remote(block, block, over_send.at[index], over_recv.at[index], scene=1 - scene).wait_recv()

    for index in range(3):
        block = olds[:, index * rows:(index + 1) * rows, :].reshape(wide, width)
        turned[index * width:(index + 1) * width, :] = block.T

    def forward(start, size):
        at = pl.ds(start, size)
        k = toks[0, :, :, at].reshape(wide, size)
        s = toks[1, :, :, at].reshape(wide, size)
        a = jnp.dot(turned[0:width, :], k, preferred_element_type=f32)
        b = jnp.dot(turned[width:2 * width, :], k, preferred_element_type=f32)
        back = -jnp.dot(turned[2 * width:3 * width, :], s, preferred_element_type=f32)
        sigma = jax.nn.sigmoid(a)
        act = a * sigma
        acts[:, at] = (act * b).astype(bf16)
        d_pre[:, 0, :, at] = (back * b * (sigma * (1.0 + a * (1.0 - sigma)))).astype(bf16).reshape(3, width // 3, size)
        d_pre[:, 1, :, at] = (back * act).astype(bf16).reshape(3, width // 3, size)

    relays = []

    def relay(index):
        inward[index].wait_recv()
        block = toks.at[:, core, :, pl.ds(tokens + index * chunk, chunk)]
        copy = remote(block, block, pass_send.at[1 + index], pass_recv.at[1 + index], hid=1 - core)
        go(copy)
        relays.append(copy)

    third = width // 3

    def gradient(part, at):
        k = toks[0, :, :, at].reshape(wide, tokens)
        s = toks[1, :, :, at].reshape(wide, tokens)
        both = contract_cols(d_pre[part, :, :, at].reshape(2 * third, tokens), k)
        down = -contract_cols(acts[part * third:(part + 1) * third, at], s)
        return both.reshape(2, third, wide), down

    swap.wait_recv()
    first, second = pl.ds(0, tokens), pl.ds(tokens, tokens)
    forward(0, 2 * chunk)
    relay(0)
    forward(2 * chunk, 2 * chunk)
    relay(2)
    for part in range(3):
        both, down = gradient(part, first)
        acc[part, 0:2] = both
        acc[part, 2] = down
    relay(1)
    relays[0].wait_recv()
    forward(tokens, chunk)
    relays[1].wait_recv()
    forward(tokens + 2 * chunk, chunk)
    relay(3)
    relays[2].wait_recv()
    forward(tokens + chunk, chunk)
    relays[3].wait_recv()
    forward(tokens + 3 * chunk, chunk)

    each = pieces // 3
    size = third // each

    def to_end(index):
        return remote(mine.at[index], from_end.at[index], end_send.at[index], end_recv.at[index], tok=same(near))

    def to_mid(index):
        return remote(mine.at[index], from_mid.at[index], mid_send.at[index], mid_recv.at[index],
                      tok=same(DEPTH - 1 - z))

    def to_fin(index):
        return remote(total.at[index], total.at[index], fin_send.at[index], fin_recv.at[index], tok=same(near))

    def local_piece(index):
        part, at = index // each, (index % each) * size
        return acc[part, :, at:at + size]

    for part in range(3):
        both, down = gradient(part, second)
        acc[part, 0:2] += both
        acc[part, 2] += down

        @pl.when(is_end)
        def _():
            for index in range(part * each, (part + 1) * each):
                mine[index] = local_piece(index).astype(bf16)
                to_end(index).start()

    ask.wait_recv()
    asked = q.at[:, core]
    ask_pass = remote(asked, asked, ask_send.at[1], ask_recv.at[1], hid=1 - core)
    go(ask_pass)

    lag = 3
    rowsum = lambda value: jnp.sum(value, axis=0, keepdims=True)
    for index in range(3):
        old = turned[index * width:(index + 1) * width, :].astype(f32)
        stats[0, 3 * index:3 * index + 1, :] = rowsum(old * old)
        stats[0, 3 * index + 1:3 * index + 3, :] = jnp.zeros((2, wide), f32)

    def tally(index):
        for matrix in range(3):
            old = turned[matrix * width + index * size:matrix * width + (index + 1) * size, :].astype(f32)
            grad = total[index, matrix].astype(f32)
            at = 3 * matrix + 1
            stats[0, at:at + 1, :] += rowsum(old * grad)
            stats[0, at + 1:at + 2, :] += rowsum(grad * grad)

    @pl.when(jnp.logical_not(is_end))
    def _():
        for turn in range(pieces + lag):
            if turn < pieces:
                to_end(turn).wait_recv()
                part, at = turn // each, (turn % each) * size
                summed = local_piece(turn) + from_end[turn].astype(f32)
                acc[part, :, at:at + size] = summed
                mine[turn] = summed.astype(bf16)
                to_mid(turn).start()
            if turn >= lag:
                index = turn - lag
                to_mid(index).wait_recv()
                total[index] = (local_piece(index) + from_mid[index].astype(f32)).astype(bf16)
                to_fin(index).start()
                tally(index)

    @pl.when(is_end)
    def _():
        for index in range(pieces):
            to_fin(index).wait_recv()
            tally(index)

    trades = []
    for index, where in enumerate(({"hid": 1 - core}, {"tok": side}, {"tok": side, "hid": 1 - core})):
        trades.append(remote(stats.at[0], stats.at[index + 1], stat_send.at[index], stat_recv.at[index], **where))
        go(trades[-1])
    ask_pass.wait_recv()
    for copy in trades:
        copy.wait_recv()
    table = (stats[0] + stats[1] + stats[2] + stats[3]) / hidden
    for index in (2, 0, 1):
        wsq, cross, gsq = (table[3 * index + i:3 * index + i + 1, :] for i in range(3))
        scale = step_ratio * jnp.sqrt(wsq) / jnp.sqrt(gsq + epsilon)
        msq = wsq - 2.0 * scale * cross + scale * scale * gsq
        grow = jnp.sqrt(wsq) / jnp.sqrt(msq + epsilon)
        old = turned[index * width:(index + 1) * width, :].astype(f32)
        grad = total[:, index].reshape(width, wide).astype(f32)
        news[index * width:(index + 1) * width, :] = ((old - scale * grad) * grow).astype(bf16)

    all_q = q[0].reshape(wide, 2 * count)
    all_g = q[1].reshape(wide, 2 * count)
    query_back = jnp.dot(news[2 * width:3 * width, :], all_g, preferred_element_type=f32)
    query_gate = jnp.dot(news[0:width, :], all_q, preferred_element_type=f32)
    query_up = jnp.dot(news[width:2 * width, :], all_q, preferred_element_type=f32)
    sigma = jax.nn.sigmoid(query_gate)
    silu = query_gate * sigma

    def hand(index, value):
        parts[index] = value.astype(bf16).reshape(2, half, 2 * count)
        copies = []
        for slot, (owner, low, where) in enumerate((
            (1 - core, 0, {"hid": 1 - core}),
            (core, count, {"tok": side}),
            (1 - core, count, {"tok": side, "hid": 1 - core}),
        )):
            copy = remote(parts.at[index, owner, :, low:low + count], got.at[index, slot],
                          part_send.at[index, slot], part_recv.at[index, slot], **where)
            copies.append(copy)
        for copy in reversed(copies):
            go(copy)
        return copies

    first_out = hand(0, contract_rows(news[2 * width:3 * width, :], (silu * query_up).astype(bf16)))
    grads = jnp.concatenate([
        (query_back * query_up * (sigma * (1.0 + query_gate * (1.0 - sigma)))).astype(bf16),
        (query_back * silu).astype(bf16),
    ], axis=0)
    second_out = hand(1, contract_rows(news[0:2 * width, :], grads))
    for index, copies in enumerate((first_out, second_out)):
        value = parts[index, core, :, 0:count].astype(f32)
        for slot, copy in enumerate(copies):
            copy.wait_recv()
            value = value + got[index, slot].astype(f32)
        result[index] = value

    for copy in sends:
        copy.wait_send()
    for part, (low, high) in enumerate(cuts):
        @pl.when(scene == part)
        def _():
            for index in range(tok - 1):
                block = olds.at[0, low:high]
                remote(block, block, old_send.at[index], old_recv.at[index], tok=side).wait_send()
                remote(block, block, over_send.at[index], over_recv.at[index], scene=1 - scene).wait_send()

    @pl.when(is_end)
    def _():
        for index in range(pieces):
            to_end(index).wait_send()

    @pl.when(jnp.logical_not(is_end))
    def _():
        for index in range(pieces):
            to_mid(index).wait_send()
            to_fin(index).wait_send()


def shards_fast(
    tok, input_keys, input_values, input_lr, gate_weight, up_weight, down_weight, queries, out_grad
):
    rows, cols = gate_weight.shape
    width = cols // 2
    tokens, half = input_keys.shape
    count = queries.shape[0]
    wide = 2 * half
    pieces = 12
    size = width // pieces
    f32, bf16, dma = jnp.float32, jnp.bfloat16, pltpu.SemaphoreType.DMA
    flow = (pieces, 3, size, wide)
    result = pl.pallas_call(
        functools.partial(whole_kernel, tok, 2 * cols, pieces),
        out_shape=jax.ShapeDtypeStruct((2, half, count), f32),
        in_specs=[HBM, HBM, VM, HBM, HBM, HBM, HBM, HBM],
        out_specs=VM,
        scratch_shapes=[
            pltpu.VMEM((2, 2, half, 2 * tokens), bf16),
            pltpu.VMEM((half, tokens), bf16),
            pltpu.VMEM((3 * rows, cols), bf16),
            pltpu.VMEM((tok, 3 * rows, width), bf16),
            pltpu.VMEM((3 * width, wide), bf16),
            pltpu.VMEM((3, 2, width // 3, 2 * tokens), bf16),
            pltpu.VMEM((width, 2 * tokens), bf16),
            pltpu.VMEM((3, 3, width // 3, wide), f32),
            pltpu.VMEM(flow, bf16),
            pltpu.VMEM(flow, bf16),
            pltpu.VMEM(flow, bf16),
            pltpu.VMEM(flow, bf16),
            pltpu.VMEM((4, 16, wide), f32),
            pltpu.VMEM((3 * width, wide), bf16),
            pltpu.VMEM((2, 2, half, 2 * count), bf16),
            pltpu.VMEM((2, 2, half, 2 * count), bf16),
            pltpu.VMEM((2, 3, half, count), bf16),
            dma((7,)), dma((tok - 1,)), dma((tok - 1,)), dma((tok - 1,)), dma((tok - 1,)),
            dma((4,)), dma((4,)), dma((5,)), dma((5,)), dma((2,)), dma((2,)),
            dma((pieces,)), dma((pieces,)), dma((pieces,)), dma((pieces,)), dma((pieces,)), dma((pieces,)),
            dma((3,)), dma((3,)), dma((2, 3)), dma((2, 3)),
        ],
        compiler_params=pltpu.CompilerParams(
            collective_id=0, has_side_effects=True, vmem_limit_bytes=60_000_000
        ),
    )(
        input_keys.T, input_values.T, input_lr.reshape(1, tokens), queries.T, out_grad.T,
        gate_weight, up_weight, down_weight,
    )
    return (result[0].astype(bf16).T, result[1].astype(bf16).T)


def fits(mesh, gate_weight, input_keys, queries):
    scene, tok, hid = (mesh.shape[name] for name in ("scene", "tok", "hid"))
    if (scene, tok, hid) != (2, WIDE * DEPTH, 2):
        return False
    depth, width = gate_weight.shape
    rows, half = depth // tok, input_keys.shape[1] // 2
    tokens, count = input_keys.shape[0] // (scene * tok), queries.shape[0] // (scene * tok)
    return (
        rows % 16 == 0 and 3 * rows > 64 and half % 16 == 0 and 2 * half == depth
        and width % (4 * 384) == 0 and tokens % 512 == 0 and count % 128 == 0
    )


def solution(mesh):
    tok = mesh.shape["tok"]
    specs = (
        P(("scene", "tok"), "hid"),
        P(("scene", "tok"), "hid"),
        P(("scene", "tok")),
        P("tok", "hid"),
        P("tok", "hid"),
        P("tok", "hid"),
        P(("scene", "tok"), "hid"),
        P(("scene", "tok"), "hid"),
    )

    def run(*args):
        fast = fits(mesh, args[3], args[0], args[6])
        shards = functools.partial(shards_fast, tok) if fast else shards_plain
        return jax.shard_map(
            shards,
            mesh=mesh,
            in_specs=specs,
            out_specs=(P(("scene", "tok"), "hid"), P(("scene", "tok"), "hid")),
            check_vma=False,
        )(*args)

    return run
```

```python
import functools

import jax
import jax.numpy as jnp
from jax import lax
from jax.experimental import pallas as pl
from jax.experimental.pallas import tpu as pltpu
from jax.sharding import PartitionSpec as P

HID = 1536


step_ratio = 0.5
epsilon = 1e-06


def silu_slope(pre):
    sigma = jax.nn.sigmoid(pre)
    return sigma * (1.0 + pre * (1.0 - sigma))


def contract_rows(left, right):
    return lax.dot_general(
        left, right, (((0,), (0,)), ((), ())), preferred_element_type=jnp.float32
    )


def contract_cols(left, right):
    return lax.dot_general(
        left, right, (((1,), (1,)), ((), ())), preferred_element_type=jnp.float32
    )


def finish(moved, wsq, msq):
    return (moved * (jnp.sqrt(wsq) / jnp.sqrt(msq + epsilon))[:, None]).astype(jnp.bfloat16)


def shards_plain(
    input_keys, input_values, input_lr, gate_weight, up_weight, down_weight, queries, out_grad
):
    keys, values = (
        lax.all_gather(input_keys, "hid", axis=1, tiled=True),
        lax.all_gather(input_values, "hid", axis=1, tiled=True),
    )
    w_gate, w_up, w_down = (
        lax.all_gather(gate_weight, "tok", axis=0, tiled=True),
        lax.all_gather(up_weight, "tok", axis=0, tiled=True),
        lax.all_gather(down_weight, "tok", axis=0, tiled=True),
    )
    scaled = (input_lr[:, None] * values.astype(jnp.float32)).astype(jnp.bfloat16)
    key_gate = jnp.dot(keys, w_gate, preferred_element_type=jnp.float32)
    key_up = jnp.dot(keys, w_up, preferred_element_type=jnp.float32)
    gate_act = jax.nn.silu(key_gate)
    key_act = (gate_act * key_up).astype(jnp.bfloat16)
    back = jnp.dot(scaled, w_down, preferred_element_type=jnp.float32)
    d_gate = (-back * key_up * silu_slope(key_gate)).astype(jnp.bfloat16)
    d_up = (-back * gate_act).astype(jnp.bfloat16)
    width = gate_weight.shape[1]
    grads = lax.psum(
        jnp.concatenate(
            [
                contract_rows(keys, d_gate),
                contract_rows(keys, d_up),
                -contract_rows(scaled, key_act),
            ],
            axis=1,
        ),
        "tok",
    )
    olds = (w_gate, w_up, w_down)
    pieces = [grads[:, :width], grads[:, width : 2 * width], grads[:, 2 * width :]]
    weights = [old.astype(jnp.float32) for old in olds]
    renewed = []
    stats = []
    for weight, grad in zip(weights, pieces):
        stats.append(jnp.sum(weight * weight, axis=1))
        stats.append(jnp.sum(weight * grad, axis=1))
        stats.append(jnp.sum(grad * grad, axis=1))
    totals = lax.psum(
        (stats[0], stats[1], stats[2], stats[3], stats[4], stats[5], stats[6], stats[7], stats[8]),
        "hid",
    )
    for index in range(3):
        wsq = totals[3 * index] / HID
        cross = totals[3 * index + 1] / HID
        gsq = totals[3 * index + 2] / HID
        scale = step_ratio * jnp.sqrt(wsq) / jnp.sqrt(gsq + epsilon)
        moved = weights[index] - scale[:, None] * pieces[index]
        msq = wsq - 2.0 * scale * cross + scale * scale * gsq
        renewed.append(finish(moved, wsq, msq))
    new_gate, new_up, new_down = (renewed[0], renewed[1], renewed[2])
    query_rows, grad_rows = (
        lax.all_gather(queries, "hid", axis=1, tiled=True),
        lax.all_gather(out_grad, "hid", axis=1, tiled=True),
    )
    query_gate = jnp.dot(query_rows, new_gate, preferred_element_type=jnp.float32)
    query_up = jnp.dot(query_rows, new_up, preferred_element_type=jnp.float32)
    query_silu = jax.nn.silu(query_gate)
    query_act = (query_silu * query_up).astype(jnp.bfloat16)
    out_part = contract_cols(query_act, new_down)
    query_back = jnp.dot(grad_rows, new_down, preferred_element_type=jnp.float32)
    q_gate_grad = (query_back * query_up * silu_slope(query_gate)).astype(jnp.bfloat16)
    q_up_grad = (query_back * query_silu).astype(jnp.bfloat16)
    grad_part = contract_cols(q_gate_grad, new_gate) + contract_cols(q_up_grad, new_up)
    out_sum, grad_sum = (
        lax.psum_scatter(
            out_part.astype(jnp.bfloat16), "hid", scatter_dimension=1, tiled=True
        ).astype(jnp.float32),
        lax.psum_scatter(
            grad_part.astype(jnp.bfloat16), "hid", scatter_dimension=1, tiled=True
        ).astype(jnp.float32),
    )
    return (out_sum.astype(jnp.bfloat16), grad_sum.astype(jnp.bfloat16))


MESH = pl.DeviceIdType.MESH
WIDE = 2
DEPTH = 4
HBM = pl.BlockSpec(memory_space=pltpu.HBM)
VM = pl.BlockSpec(memory_space=pltpu.VMEM)


def remote(src, dst, send, recv, **where):
    return pltpu.make_async_remote_copy(
        src_ref=src, dst_ref=dst, send_sem=send, recv_sem=recv,
        device_id=where, device_id_type=MESH,
    )


def bend(level):
    return 0


def chip_of(level, color):
    return level * WIDE + lax.rem(color + bend(level), 2)


def whole_kernel(
    tok, hidden, pieces,
    keys_in, vals_in, lr, q_in, g_in, gate_in, up_in, down_in,
    result,
    toks, vraw, own, olds, turned, d_pre, acts, acc, mine, from_end, from_mid, total,
    stats, news, flips, q, parts, give, got,
    local, hop_send, hop_recv, run_send, run_recv, over_send, over_recv,
    tok_send, tok_recv, pass_send, pass_recv, ask_send, ask_recv,
    end_send, end_recv, mid_send, mid_recv, fin_send, fin_recv,
    stat_send, stat_recv, part_send, part_recv,
):
    f32, bf16 = jnp.float32, jnp.bfloat16
    scene, core, rank = lax.axis_index("scene"), lax.axis_index("hid"), lax.axis_index("tok")
    z, x = lax.div(rank, WIDE), lax.rem(rank, WIDE)
    color = lax.rem(x + bend(z), 2)
    rows = gate_in.shape[0]
    half, tokens = keys_in.shape
    count = q_in.shape[1]
    width = olds.shape[2]
    wide = 2 * half
    near = z + 1 - 2 * lax.rem(z, 2)
    side = z * WIDE + 1 - x
    stack = near * WIDE + x
    is_end = (z == 0) | (z == DEPTH - 1)

    def same(level):
        return chip_of(level, color)

    barrier = pltpu.get_barrier_semaphore()
    peers = [{"hid": 1 - core}, {"scene": 1 - scene}, {"tok": side}, {"tok": side, "hid": 1 - core}]
    for where in peers:
        pl.semaphore_signal(barrier, inc=1, device_id=where, device_id_type=MESH)

    @pl.when(z > 0)
    def _():
        pl.semaphore_signal(barrier, inc=1, device_id={"tok": same(z - 1)}, device_id_type=MESH)

    @pl.when(z < DEPTH - 1)
    def _():
        pl.semaphore_signal(barrier, inc=1, device_id={"tok": same(z + 1)}, device_id_type=MESH)

    loads = []
    for index, (src, dst) in enumerate((
        (gate_in, own.at[0:rows]),
        (up_in, own.at[rows:2 * rows]),
        (down_in, own.at[2 * rows:3 * rows]),
        (vals_in, vraw),
        (keys_in, toks.at[0, core, :, 0:tokens]),
        (q_in, q.at[0, core, :, 0:count]),
        (g_in, q.at[1, core, :, 0:count]),
    )):
        loads.append(pltpu.make_async_copy(src, dst, local.at[index]))
        loads[-1].start()
    for load in loads[:4]:
        load.wait()
    toks[1, core, :, 0:tokens] = (lr[...] * vraw[...].astype(f32)).astype(bf16)

    @pl.when(is_end)
    def _():
        pl.semaphore_wait(barrier, len(peers) + 1)

    @pl.when(jnp.logical_not(is_end))
    def _():
        pl.semaphore_wait(barrier, len(peers) + 2)

    sends = []

    def go(copy):
        copy.start()
        sends.append(copy)

    mycols = pl.ds(pl.multiple_of(color * width, width), width)
    sidecols = pl.ds(pl.multiple_of((1 - color) * width, width), width)
    strips = [slice(index * rows, (index + 1) * rows) for index in range(3)]
    leads = color == scene

    def hop(m):
        return remote(own.at[strips[m], sidecols], olds.at[rank, strips[m]], hop_send.at[m], hop_recv.at[m], tok=side)

    def run(m, level, way, src=None):
        dst = olds.at[chip_of(level, scene), strips[m]]
        target = z + 1 if way == 0 else z - 1
        return remote(dst if src is None else src, dst, run_send.at[m, way, level], run_recv.at[m, level],
                      tok=same(target))

    def over(m, level):
        block = olds.at[chip_of(level, scene), strips[m]]
        return remote(block, block, over_send.at[m, level], over_recv.at[m, level], scene=1 - scene)

    def launch(m, src):
        @pl.when(z < DEPTH - 1)
        def _():
            run(m, z, 0, src).start()

        @pl.when(z > 0)
        def _():
            run(m, z, 1, src).start()

    def came(m, level, way):
        run(m, level, way).wait_recv()
        over(m, level).start()

    for m in range(3):
        go(hop(m))

        @pl.when(leads)
        def _():
            launch(m, own.at[strips[m], mycols])

    for load in loads[4:]:
        load.wait()
    swap = remote(toks.at[:, core, :, 0:tokens], toks.at[:, core, :, 0:tokens],
                  pass_send.at[0], pass_recv.at[0], hid=1 - core)
    go(swap)

    unit = tokens // 8
    spans = ((0, 3), (3, 2), (5, 2), (7, 1))
    inward = []
    for index, (low, size) in enumerate(spans):
        at = pl.ds(low * unit, size * unit)
        to = pl.ds(tokens + low * unit, size * unit)
        inward.append(remote(toks.at[:, core, :, at], toks.at[:, core, :, to],
                             tok_send.at[index], tok_recv.at[index], tok=side))
        go(inward[index])
    olds[rank] = own[:, mycols]

    @pl.when(jnp.logical_not(leads))
    def _():
        for m in range(3):
            block = olds.at[side, strips[m]]
            remote(block, block, hop_send.at[m], hop_recv.at[m], tok=side).wait_recv()
            launch(m, block)

    for step in range(1, DEPTH):
        for m in range(3):
            @pl.when(z >= step)
            def _():
                came(m, z - step, 0)

                @pl.when(z < DEPTH - 1)
                def _():
                    run(m, z - step, 0).start()

            @pl.when(z + step < DEPTH)
            def _():
                came(m, z + step, 1)

                @pl.when(z > 0)
                def _():
                    run(m, z + step, 1).start()

    @pl.when(leads)
    def _():
        for m in range(3):
            block = olds.at[side, strips[m]]
            remote(block, block, hop_send.at[m], hop_recv.at[m], tok=side).wait_recv()

    for step in range(1, DEPTH):
        for m in range(3):
            level = lax.rem(z + step, DEPTH)
            block = olds.at[chip_of(level, 1 - scene), strips[m]]
            remote(block, block, over_send.at[m, level], over_recv.at[m, level], scene=1 - scene).wait_recv()

    for index in range(3):
        block = olds[:, index * rows:(index + 1) * rows, :].reshape(wide, width)
        turned[index * width:(index + 1) * width, :] = block.T

    def forward(start, size):
        at = pl.ds(start, size)
        k = toks[0, :, :, at].reshape(wide, size)
        s = toks[1, :, :, at].reshape(wide, size)
        a = jnp.dot(turned[0:width, :], k, preferred_element_type=f32)
        b = jnp.dot(turned[width:2 * width, :], k, preferred_element_type=f32)
        back = -jnp.dot(turned[2 * width:3 * width, :], s, preferred_element_type=f32)
        sigma = jax.nn.sigmoid(a)
        act = a * sigma
        acts[:, at] = (act * b).astype(bf16)
        d_pre[:, 0, :, at] = (back * b * (sigma * (1.0 + a * (1.0 - sigma)))).astype(bf16).reshape(3, width // 3, size)
        d_pre[:, 1, :, at] = (back * act).astype(bf16).reshape(3, width // 3, size)

    relays = []

    def relay(index):
        inward[index].wait_recv()
        low, size = spans[index]
        block = toks.at[:, core, :, pl.ds(tokens + low * unit, size * unit)]
        copy = remote(block, block, pass_send.at[1 + index], pass_recv.at[1 + index], hid=1 - core)
        go(copy)
        relays.append(copy)

    third = width // 3

    def gradient(part, at):
        k = toks[0, :, :, at].reshape(wide, tokens)
        s = toks[1, :, :, at].reshape(wide, tokens)
        both = contract_cols(d_pre[part, :, :, at].reshape(2 * third, tokens), k)
        down = -contract_cols(acts[part * third:(part + 1) * third, at], s)
        return both.reshape(2, third, wide), down

    swap.wait_recv()
    first, second = pl.ds(0, tokens), pl.ds(tokens, tokens)
    half_tokens = tokens // 2
    forward(0, half_tokens)
    relay(0)
    forward(half_tokens, half_tokens)
    relay(1)
    for part in range(3):
        both, down = gradient(part, first)
        acc[part, 0:2] = both
        acc[part, 2] = down
    relays[0].wait_recv()
    forward(tokens, 3 * unit)
    relay(2)
    relays[1].wait_recv()
    forward(tokens + 3 * unit, 2 * unit)
    relay(3)
    ask = remote(q.at[:, core, :, 0:count], q.at[:, core, :, count:2 * count],
                 ask_send.at[0], ask_recv.at[0], tok=side)
    go(ask)
    relays[2].wait_recv()
    forward(tokens + 5 * unit, 2 * unit)
    relays[3].wait_recv()
    forward(tokens + 7 * unit, unit)

    each = pieces // 3
    size = third // each

    def to_end(index):
        return remote(mine.at[index], from_end.at[index], end_send.at[index], end_recv.at[index], tok=same(near))

    def to_mid(index):
        return remote(mine.at[index], from_mid.at[index], mid_send.at[index], mid_recv.at[index],
                      tok=same(DEPTH - 1 - z))

    def to_fin(index):
        return remote(total.at[index], total.at[index], fin_send.at[index], fin_recv.at[index], tok=same(near))

    def local_piece(index):
        part, at = index // each, (index % each) * size
        return acc[part, :, at:at + size]

    for part in range(3):
        both, down = gradient(part, second)
        acc[part, 0:2] += both
        acc[part, 2] += down

        @pl.when(is_end)
        def _():
            for index in range(part * each, (part + 1) * each):
                mine[index] = local_piece(index).astype(bf16)
                to_end(index).start()

    ask.wait_recv()
    asked = q.at[:, core]
    ask_pass = remote(asked, asked, ask_send.at[1], ask_recv.at[1], hid=1 - core)
    go(ask_pass)

    lag = 5
    rowsum = lambda value: jnp.sum(value, axis=0, keepdims=True)
    for index in range(3):
        old = turned[index * width:(index + 1) * width, :].astype(f32)
        stats[0, 3 * index:3 * index + 1, :] = rowsum(old * old)
        stats[0, 3 * index + 1:3 * index + 3, :] = jnp.zeros((2, wide), f32)

    def tally(index):
        for matrix in range(3):
            old = turned[matrix * width + index * size:matrix * width + (index + 1) * size, :].astype(f32)
            grad = total[index, matrix].astype(f32)
            at = 3 * matrix + 1
            stats[0, at:at + 1, :] += rowsum(old * grad)
            stats[0, at + 1:at + 2, :] += rowsum(grad * grad)

    @pl.when(jnp.logical_not(is_end))
    def _():
        for turn in range(pieces + lag):
            if turn < pieces:
                to_end(turn).wait_recv()
                part, at = turn // each, (turn % each) * size
                summed = local_piece(turn) + from_end[turn].astype(f32)
                acc[part, :, at:at + size] = summed
                mine[turn] = summed.astype(bf16)
                to_mid(turn).start()
            if turn >= lag:
                index = turn - lag
                to_mid(index).wait_recv()
                total[index] = (local_piece(index) + from_mid[index].astype(f32)).astype(bf16)
                to_fin(index).start()
                tally(index)

    @pl.when(is_end)
    def _():
        for index in range(pieces):
            to_fin(index).wait_recv()
            tally(index)

    trades = []
    for index, where in enumerate(({"hid": 1 - core}, {"tok": side}, {"tok": side, "hid": 1 - core})):
        trades.append(remote(stats.at[0], stats.at[index + 1], stat_send.at[index], stat_recv.at[index], **where))
        go(trades[-1])
    ask_pass.wait_recv()
    for copy in trades:
        copy.wait_recv()
    table = (stats[0] + stats[1] + stats[2] + stats[3]) / hidden
    for index in (2, 0, 1):
        wsq, cross, gsq = (table[3 * index + i:3 * index + i + 1, :] for i in range(3))
        scale = step_ratio * jnp.sqrt(wsq) / jnp.sqrt(gsq + epsilon)
        msq = wsq - 2.0 * scale * cross + scale * scale * gsq
        grow = jnp.sqrt(wsq) / jnp.sqrt(msq + epsilon)
        old = turned[index * width:(index + 1) * width, :].astype(f32)
        grad = total[:, index].reshape(width, wide).astype(f32)
        news[index * width:(index + 1) * width, :] = ((old - scale * grad) * grow).astype(bf16)

    for index in range(3):
        flips[:, index * width:(index + 1) * width] = news[index * width:(index + 1) * width, :].T

    def answer(slot):
        low = slot * count
        all_q = q[0, :, :, low:low + count].reshape(wide, count)
        all_g = q[1, :, :, low:low + count].reshape(wide, count)
        both = jnp.dot(news[0:2 * width, :], all_q, preferred_element_type=f32)
        query_back = jnp.dot(news[2 * width:3 * width, :], all_g, preferred_element_type=f32)
        query_gate, query_up = both[0:width], both[width:2 * width]
        sigma = jax.nn.sigmoid(query_gate)
        silu = query_gate * sigma
        act = (silu * query_up).astype(bf16)
        grads = jnp.concatenate([
            (query_back * query_up * (sigma * (1.0 + query_gate * (1.0 - sigma)))).astype(bf16),
            (query_back * silu).astype(bf16),
        ], axis=0)
        first = jnp.dot(flips[:, 2 * width:3 * width], act, preferred_element_type=f32)
        second = jnp.dot(flips[:, 0:2 * width], grads, preferred_element_type=f32)
        parts[slot, :, 0] = first.reshape(2, half, count)
        parts[slot, :, 1] = second.reshape(2, half, count)
        give[slot] = parts[slot, 1 - core].astype(bf16)
        copy = remote(give.at[slot], got.at[slot], part_send.at[slot], part_recv.at[slot], hid=1 - core)
        go(copy)
        return copy

    away = answer(1)
    here = answer(0)
    away.wait_recv()
    give[2] = (parts[1, core] + got[1].astype(f32)).astype(bf16)
    back = remote(give.at[2], got.at[2], part_send.at[2], part_recv.at[2], tok=side)
    go(back)
    here.wait_recv()
    value = parts[0, core] + got[0].astype(f32)
    back.wait_recv()
    result[...] = value + got[2].astype(f32)

    for copy in sends:
        copy.wait_send()
    for level in range(DEPTH):
        for m in range(3):
            @pl.when((z >= level) & (z < DEPTH - 1))
            def _():
                run(m, level, 0).wait_send()

            @pl.when((z <= level) & (z > 0))
            def _():
                run(m, level, 1).wait_send()

            @pl.when(z != level)
            def _():
                over(m, level).wait_send()

    @pl.when(is_end)
    def _():
        for index in range(pieces):
            to_end(index).wait_send()

    @pl.when(jnp.logical_not(is_end))
    def _():
        for index in range(pieces):
            to_mid(index).wait_send()
            to_fin(index).wait_send()


def shards_fast(
    tok, input_keys, input_values, input_lr, gate_weight, up_weight, down_weight, queries, out_grad
):
    rows, cols = gate_weight.shape
    width = cols // 2
    tokens, half = input_keys.shape
    count = queries.shape[0]
    wide = 2 * half
    pieces = 24
    size = width // pieces
    f32, bf16, dma = jnp.float32, jnp.bfloat16, pltpu.SemaphoreType.DMA
    flow = (pieces, 3, size, wide)
    result = pl.pallas_call(
        functools.partial(whole_kernel, tok, 2 * cols, pieces),
        out_shape=jax.ShapeDtypeStruct((2, half, count), f32),
        in_specs=[HBM, HBM, VM, HBM, HBM, HBM, HBM, HBM],
        out_specs=VM,
        scratch_shapes=[
            pltpu.VMEM((2, 2, half, 2 * tokens), bf16),
            pltpu.VMEM((half, tokens), bf16),
            pltpu.VMEM((3 * rows, cols), bf16),
            pltpu.VMEM((tok, 3 * rows, width), bf16),
            pltpu.VMEM((3 * width, wide), bf16),
            pltpu.VMEM((3, 2, width // 3, 2 * tokens), bf16),
            pltpu.VMEM((width, 2 * tokens), bf16),
            pltpu.VMEM((3, 3, width // 3, wide), f32),
            pltpu.VMEM(flow, bf16),
            pltpu.VMEM(flow, bf16),
            pltpu.VMEM(flow, bf16),
            pltpu.VMEM(flow, bf16),
            pltpu.VMEM((4, 16, wide), f32),
            pltpu.VMEM((3 * width, wide), bf16),
            pltpu.VMEM((wide, 3 * width), bf16),
            pltpu.VMEM((2, 2, half, 2 * count), bf16),
            pltpu.VMEM((2, 2, 2, half, count), f32),
            pltpu.VMEM((3, 2, half, count), bf16),
            pltpu.VMEM((3, 2, half, count), bf16),
            dma((7,)), dma((3,)), dma((3,)), dma((3, 2, DEPTH)), dma((3, DEPTH)), dma((3, DEPTH)), dma((3, DEPTH)),
            dma((4,)), dma((4,)), dma((5,)), dma((5,)), dma((2,)), dma((2,)),
            dma((pieces,)), dma((pieces,)), dma((pieces,)), dma((pieces,)), dma((pieces,)), dma((pieces,)),
            dma((3,)), dma((3,)), dma((3,)), dma((3,)),
        ],
        compiler_params=pltpu.CompilerParams(
            collective_id=0, has_side_effects=True, vmem_limit_bytes=60_000_000
        ),
    )(
        input_keys.T, input_values.T, input_lr.reshape(1, tokens), queries.T, out_grad.T,
        gate_weight, up_weight, down_weight,
    )
    return (result[0].astype(bf16).T, result[1].astype(bf16).T)


def fits(mesh, gate_weight, input_keys, queries):
    scene, tok, hid = (mesh.shape[name] for name in ("scene", "tok", "hid"))
    if (scene, tok, hid) != (2, WIDE * DEPTH, 2):
        return False
    depth, width = gate_weight.shape
    rows, half = depth // tok, input_keys.shape[1] // 2
    tokens, count = input_keys.shape[0] // (scene * tok), queries.shape[0] // (scene * tok)
    return (
        rows % 16 == 0 and half % 16 == 0 and 2 * half == depth
        and width % 1536 == 0 and tokens % 1024 == 0 and count % 128 == 0
    )


def solution(mesh):
    tok = mesh.shape["tok"]
    specs = (
        P(("scene", "tok"), "hid"),
        P(("scene", "tok"), "hid"),
        P(("scene", "tok")),
        P("tok", "hid"),
        P("tok", "hid"),
        P("tok", "hid"),
        P(("scene", "tok"), "hid"),
        P(("scene", "tok"), "hid"),
    )

    def run(*args):
        fast = fits(mesh, args[3], args[0], args[6])
        shards = functools.partial(shards_fast, tok) if fast else shards_plain
        return jax.shard_map(
            shards,
            mesh=mesh,
            in_specs=specs,
            out_specs=(P(("scene", "tok"), "hid"), P(("scene", "tok"), "hid")),
            check_vma=False,
        )(*args)

    return run
```

```python
import functools

import jax
import jax.numpy as jnp
from jax import lax
from jax.experimental import pallas as pl
from jax.experimental.pallas import tpu as pltpu
from jax.sharding import PartitionSpec as P

HID = 1536


step_ratio = 0.5
epsilon = 1e-06


def silu_slope(pre):
    sigma = jax.nn.sigmoid(pre)
    return sigma * (1.0 + pre * (1.0 - sigma))


def contract_rows(left, right):
    return lax.dot_general(
        left, right, (((0,), (0,)), ((), ())), preferred_element_type=jnp.float32
    )


def contract_cols(left, right):
    return lax.dot_general(
        left, right, (((1,), (1,)), ((), ())), preferred_element_type=jnp.float32
    )


def finish(moved, wsq, msq):
    return (moved * (jnp.sqrt(wsq) / jnp.sqrt(msq + epsilon))[:, None]).astype(jnp.bfloat16)


def shards_plain(
    input_keys, input_values, input_lr, gate_weight, up_weight, down_weight, queries, out_grad
):
    keys, values = (
        lax.all_gather(input_keys, "hid", axis=1, tiled=True),
        lax.all_gather(input_values, "hid", axis=1, tiled=True),
    )
    w_gate, w_up, w_down = (
        lax.all_gather(gate_weight, "tok", axis=0, tiled=True),
        lax.all_gather(up_weight, "tok", axis=0, tiled=True),
        lax.all_gather(down_weight, "tok", axis=0, tiled=True),
    )
    scaled = (input_lr[:, None] * values.astype(jnp.float32)).astype(jnp.bfloat16)
    key_gate = jnp.dot(keys, w_gate, preferred_element_type=jnp.float32)
    key_up = jnp.dot(keys, w_up, preferred_element_type=jnp.float32)
    gate_act = jax.nn.silu(key_gate)
    key_act = (gate_act * key_up).astype(jnp.bfloat16)
    back = jnp.dot(scaled, w_down, preferred_element_type=jnp.float32)
    d_gate = (-back * key_up * silu_slope(key_gate)).astype(jnp.bfloat16)
    d_up = (-back * gate_act).astype(jnp.bfloat16)
    width = gate_weight.shape[1]
    grads = lax.psum(
        jnp.concatenate(
            [
                contract_rows(keys, d_gate),
                contract_rows(keys, d_up),
                -contract_rows(scaled, key_act),
            ],
            axis=1,
        ),
        "tok",
    )
    olds = (w_gate, w_up, w_down)
    pieces = [grads[:, :width], grads[:, width : 2 * width], grads[:, 2 * width :]]
    weights = [old.astype(jnp.float32) for old in olds]
    renewed = []
    stats = []
    for weight, grad in zip(weights, pieces):
        stats.append(jnp.sum(weight * weight, axis=1))
        stats.append(jnp.sum(weight * grad, axis=1))
        stats.append(jnp.sum(grad * grad, axis=1))
    totals = lax.psum(
        (stats[0], stats[1], stats[2], stats[3], stats[4], stats[5], stats[6], stats[7], stats[8]),
        "hid",
    )
    for index in range(3):
        wsq = totals[3 * index] / HID
        cross = totals[3 * index + 1] / HID
        gsq = totals[3 * index + 2] / HID
        scale = step_ratio * jnp.sqrt(wsq) / jnp.sqrt(gsq + epsilon)
        moved = weights[index] - scale[:, None] * pieces[index]
        msq = wsq - 2.0 * scale * cross + scale * scale * gsq
        renewed.append(finish(moved, wsq, msq))
    new_gate, new_up, new_down = (renewed[0], renewed[1], renewed[2])
    query_rows, grad_rows = (
        lax.all_gather(queries, "hid", axis=1, tiled=True),
        lax.all_gather(out_grad, "hid", axis=1, tiled=True),
    )
    query_gate = jnp.dot(query_rows, new_gate, preferred_element_type=jnp.float32)
    query_up = jnp.dot(query_rows, new_up, preferred_element_type=jnp.float32)
    query_silu = jax.nn.silu(query_gate)
    query_act = (query_silu * query_up).astype(jnp.bfloat16)
    out_part = contract_cols(query_act, new_down)
    query_back = jnp.dot(grad_rows, new_down, preferred_element_type=jnp.float32)
    q_gate_grad = (query_back * query_up * silu_slope(query_gate)).astype(jnp.bfloat16)
    q_up_grad = (query_back * query_silu).astype(jnp.bfloat16)
    grad_part = contract_cols(q_gate_grad, new_gate) + contract_cols(q_up_grad, new_up)
    out_sum, grad_sum = (
        lax.psum_scatter(
            out_part.astype(jnp.bfloat16), "hid", scatter_dimension=1, tiled=True
        ).astype(jnp.float32),
        lax.psum_scatter(
            grad_part.astype(jnp.bfloat16), "hid", scatter_dimension=1, tiled=True
        ).astype(jnp.float32),
    )
    return (out_sum.astype(jnp.bfloat16), grad_sum.astype(jnp.bfloat16))


MESH = pl.DeviceIdType.MESH
WIDE = 2
DEPTH = 4
HBM = pl.BlockSpec(memory_space=pltpu.HBM)
VM = pl.BlockSpec(memory_space=pltpu.VMEM)


def remote(src, dst, send, recv, **where):
    return pltpu.make_async_remote_copy(
        src_ref=src, dst_ref=dst, send_sem=send, recv_sem=recv,
        device_id=where, device_id_type=MESH,
    )


def bend(level):
    return 0


def chip_of(level, color):
    return level * WIDE + lax.rem(color + bend(level), 2)


def whole_kernel(
    tok, hidden, pieces,
    keys_in, vals_in, lr_in, q_in, g_in, gate_in, up_in, down_in,
    result,
    toks, vraw, lr, own, olds, turned, d_pre, acts, acc, mine, from_end, from_mid, total,
    stats, tallies, news, flips, q, parts, give, got,
    local, hop_send, hop_recv, run_send, run_recv, over_send, over_recv,
    tok_send, tok_recv, pass_send, pass_recv, ask_send, ask_recv,
    end_send, end_recv, mid_send, mid_recv, fin_send, fin_recv,
    stat_send, stat_recv, part_send, part_recv,
):
    f32, bf16 = jnp.float32, jnp.bfloat16
    scene, core, rank = lax.axis_index("scene"), lax.axis_index("hid"), lax.axis_index("tok")
    z, x = lax.div(rank, WIDE), lax.rem(rank, WIDE)
    color = lax.rem(x + bend(z), 2)
    rows = gate_in.shape[0]
    half, tokens = keys_in.shape
    count = q_in.shape[1]
    width = olds.shape[2]
    wide = 2 * half
    near = z + 1 - 2 * lax.rem(z, 2)
    side = z * WIDE + 1 - x
    stack = near * WIDE + x
    is_end = (z == 0) | (z == DEPTH - 1)

    def same(level):
        return chip_of(level, color)

    barrier = pltpu.get_barrier_semaphore()
    peers = [{"hid": 1 - core}, {"scene": 1 - scene}, {"tok": side}, {"tok": side, "hid": 1 - core}]
    across = near * WIDE + 1 - x
    peers += [{"tok": same(near), "hid": 1 - core}, {"tok": across}, {"tok": across, "hid": 1 - core}]
    for where in peers:
        pl.semaphore_signal(barrier, inc=1, device_id=where, device_id_type=MESH)

    @pl.when(z > 0)
    def _():
        pl.semaphore_signal(barrier, inc=1, device_id={"tok": same(z - 1)}, device_id_type=MESH)

    @pl.when(z < DEPTH - 1)
    def _():
        pl.semaphore_signal(barrier, inc=1, device_id={"tok": same(z + 1)}, device_id_type=MESH)

    loads = []
    for index, (src, dst) in enumerate((
        (gate_in, own.at[0:rows]),
        (up_in, own.at[rows:2 * rows]),
        (down_in, own.at[2 * rows:3 * rows]),
        (vals_in, vraw),
        (lr_in, lr),
        (keys_in, toks.at[0, core, :, 0:tokens]),
        (q_in, q.at[0, core, :, 0:count]),
        (g_in, q.at[1, core, :, 0:count]),
    )):
        loads.append(pltpu.make_async_copy(src, dst, local.at[index]))
        loads[-1].start()
    for load in loads[:5]:
        load.wait()
    toks[1, core, :, 0:tokens] = (lr[...] * vraw[...].astype(f32)).astype(bf16)

    @pl.when(is_end)
    def _():
        pl.semaphore_wait(barrier, len(peers) + 1)

    @pl.when(jnp.logical_not(is_end))
    def _():
        pl.semaphore_wait(barrier, len(peers) + 2)

    sends = []

    def go(copy):
        copy.start()
        sends.append(copy)

    mycols = pl.ds(pl.multiple_of(color * width, width), width)
    sidecols = pl.ds(pl.multiple_of((1 - color) * width, width), width)
    strips = [slice(index * rows, (index + 1) * rows) for index in range(3)]
    leads = color == scene

    def hop(m):
        return remote(own.at[strips[m], sidecols], olds.at[rank, strips[m]], hop_send.at[m], hop_recv.at[m], tok=side)

    def run(m, level, way, src=None):
        dst = olds.at[chip_of(level, scene), strips[m]]
        target = z + 1 if way == 0 else z - 1
        return remote(dst if src is None else src, dst, run_send.at[m, way, level], run_recv.at[m, level],
                      tok=same(target))

    def over(m, level):
        block = olds.at[chip_of(level, scene), strips[m]]
        return remote(block, block, over_send.at[m, level], over_recv.at[m, level], scene=1 - scene)

    def launch(m, src):
        @pl.when(z < DEPTH - 1)
        def _():
            run(m, z, 0, src).start()

        @pl.when(z > 0)
        def _():
            run(m, z, 1, src).start()

    def came(m, level, way):
        run(m, level, way).wait_recv()
        over(m, level).start()

    for m in range(3):
        go(hop(m))

        @pl.when(leads)
        def _():
            launch(m, own.at[strips[m], mycols])

    for load in loads[5:]:
        load.wait()
    swap = remote(toks.at[:, core, :, 0:tokens], toks.at[:, core, :, 0:tokens],
                  pass_send.at[0], pass_recv.at[0], hid=1 - core)
    go(swap)

    unit = tokens // 8
    spans = ((0, 3), (3, 2), (5, 2), (7, 1))
    inward = []
    for index, (low, size) in enumerate(spans):
        at = pl.ds(low * unit, size * unit)
        to = pl.ds(tokens + low * unit, size * unit)
        inward.append(remote(toks.at[:, core, :, at], toks.at[:, core, :, to],
                             tok_send.at[index], tok_recv.at[index], tok=side))
        go(inward[index])
    olds[rank] = own[:, mycols]

    @pl.when(jnp.logical_not(leads))
    def _():
        for m in range(3):
            block = olds.at[side, strips[m]]
            remote(block, block, hop_send.at[m], hop_recv.at[m], tok=side).wait_recv()
            launch(m, block)

    for step in range(1, DEPTH):
        for m in range(3):
            @pl.when(z >= step)
            def _():
                came(m, z - step, 0)

                @pl.when(z < DEPTH - 1)
                def _():
                    run(m, z - step, 0).start()

            @pl.when(z + step < DEPTH)
            def _():
                came(m, z + step, 1)

                @pl.when(z > 0)
                def _():
                    run(m, z + step, 1).start()

    @pl.when(leads)
    def _():
        for m in range(3):
            block = olds.at[side, strips[m]]
            remote(block, block, hop_send.at[m], hop_recv.at[m], tok=side).wait_recv()

    for step in range(1, DEPTH):
        for m in range(3):
            level = lax.rem(z + step, DEPTH)
            block = olds.at[chip_of(level, 1 - scene), strips[m]]
            remote(block, block, over_send.at[m, level], over_recv.at[m, level], scene=1 - scene).wait_recv()

    for index in range(3):
        block = olds[:, index * rows:(index + 1) * rows, :].reshape(wide, width)
        turned[index * width:(index + 1) * width, :] = block.T

    def forward(start, size):
        at = pl.ds(start, size)
        k = toks[0, :, :, at].reshape(wide, size)
        s = toks[1, :, :, at].reshape(wide, size)
        a = jnp.dot(turned[0:width, :], k, preferred_element_type=f32)
        b = jnp.dot(turned[width:2 * width, :], k, preferred_element_type=f32)
        back = -jnp.dot(turned[2 * width:3 * width, :], s, preferred_element_type=f32)
        sigma = jax.nn.sigmoid(a)
        act = a * sigma
        acts[:, at] = (act * b).astype(bf16)
        d_pre[:, 0, :, at] = (back * b * (sigma * (1.0 + a * (1.0 - sigma)))).astype(bf16).reshape(3, width // 3, size)
        d_pre[:, 1, :, at] = (back * act).astype(bf16).reshape(3, width // 3, size)

    relays = []

    def relay(index):
        inward[index].wait_recv()
        low, size = spans[index]
        block = toks.at[:, core, :, pl.ds(tokens + low * unit, size * unit)]
        copy = remote(block, block, pass_send.at[1 + index], pass_recv.at[1 + index], hid=1 - core)
        go(copy)
        relays.append(copy)

    third = width // 3

    def gradient(part, at):
        k = toks[0, :, :, at].reshape(wide, tokens)
        s = toks[1, :, :, at].reshape(wide, tokens)
        both = contract_cols(d_pre[part, :, :, at].reshape(2 * third, tokens), k)
        down = -contract_cols(acts[part * third:(part + 1) * third, at], s)
        return both.reshape(2, third, wide), down

    swap.wait_recv()
    first, second = pl.ds(0, tokens), pl.ds(tokens, tokens)
    half_tokens = tokens // 2
    forward(0, half_tokens)
    relay(0)
    forward(half_tokens, half_tokens)
    relay(1)
    for part in range(3):
        both, down = gradient(part, first)
        acc[part, 0:2] = both
        acc[part, 2] = down
    relays[0].wait_recv()
    forward(tokens, 3 * unit)
    relay(2)
    relays[1].wait_recv()
    forward(tokens + 3 * unit, 2 * unit)
    relay(3)
    ask = remote(q.at[:, core, :, 0:count], q.at[:, core, :, count:2 * count],
                 ask_send.at[0], ask_recv.at[0], tok=side)
    go(ask)
    relays[2].wait_recv()
    forward(tokens + 5 * unit, 2 * unit)
    relays[3].wait_recv()
    forward(tokens + 7 * unit, unit)

    each = pieces // 3
    size = third // each

    def to_end(index):
        return remote(mine.at[index], from_end.at[index], end_send.at[index], end_recv.at[index], tok=same(near))

    def to_mid(index):
        return remote(mine.at[index], from_mid.at[index], mid_send.at[index], mid_recv.at[index],
                      tok=same(DEPTH - 1 - z))

    def to_fin(index):
        return remote(total.at[index], total.at[index], fin_send.at[index], fin_recv.at[index], tok=same(near))

    def local_piece(index):
        part, at = index // each, (index % each) * size
        return acc[part, :, at:at + size]

    for part in range(3):
        both, down = gradient(part, second)
        acc[part, 0:2] += both
        acc[part, 2] += down

        @pl.when(is_end)
        def _():
            for index in range(part * each, (part + 1) * each):
                mine[index] = local_piece(index).astype(bf16)
                to_end(index).start()

    ask.wait_recv()
    asked = q.at[:, core]
    ask_pass = remote(asked, asked, ask_send.at[1], ask_recv.at[1], hid=1 - core)
    go(ask_pass)

    lag = 3
    rowsum = lambda value: jnp.sum(value, axis=0, keepdims=True)

    def tally(index):
        for matrix in range(3):
            old = turned[matrix * width + index * size:matrix * width + (index + 1) * size, :].astype(f32)
            grad = total[index, matrix].astype(f32)
            tallies[2 * matrix] += jnp.sum((old * grad).reshape(size // 8, 8, wide), axis=0)
            tallies[2 * matrix + 1] += jnp.sum((grad * grad).reshape(size // 8, 8, wide), axis=0)

    def trade(index):
        dx, dc = (index // 2) % 2, index % 2
        level = z if index < 4 else near
        where = {"tok": level * WIDE + (1 - x if dx else x)}
        if dc:
            where["hid"] = 1 - core
        slot = 2 * dx + dc
        return remote(stats.at[0], stats.at[slot], stat_send.at[index], stat_recv.at[slot], **where)

    @pl.when(jnp.logical_not(is_end))
    def _():
        tallies[...] = jnp.zeros_like(tallies)
        for index in range(3):
            old = turned[index * width:(index + 1) * width, :].astype(f32)
            stats[0, 3 * index:3 * index + 1, :] = rowsum(old * old)
        for turn in range(pieces + lag):
            if turn < pieces:
                to_end(turn).wait_recv()
                part, at = turn // each, (turn % each) * size
                summed = local_piece(turn) + from_end[turn].astype(f32)
                acc[part, :, at:at + size] = summed
                mine[turn] = summed.astype(bf16)
                to_mid(turn).start()
            if turn >= lag:
                index = turn - lag
                to_mid(index).wait_recv()
                total[index] = (local_piece(index) + from_mid[index].astype(f32)).astype(bf16)
                to_fin(index).start()
                tally(index)

        for index in range(3):
            for kind in range(2):
                at = 3 * index + 1 + kind
                stats[0, at:at + 1, :] = rowsum(tallies[2 * index + kind])
        for index in (7, 6, 5, 4, 3, 2, 1):
            trade(index).start()
        for index in (1, 2, 3):
            trade(index).wait_recv()

    @pl.when(is_end)
    def _():
        for index in range(pieces):
            to_fin(index).wait_recv()
        for index in range(4):
            trade(index).wait_recv()

    ask_pass.wait_recv()
    table = (stats[0] + stats[1] + stats[2] + stats[3]) / hidden
    for index in (2, 0, 1):
        wsq, cross, gsq = (table[3 * index + i:3 * index + i + 1, :] for i in range(3))
        scale = step_ratio * jnp.sqrt(wsq) / jnp.sqrt(gsq + epsilon)
        msq = wsq - 2.0 * scale * cross + scale * scale * gsq
        grow = jnp.sqrt(wsq) / jnp.sqrt(msq + epsilon)
        old = turned[index * width:(index + 1) * width, :].astype(f32)
        grad = total[:, index].reshape(width, wide).astype(f32)
        news[index * width:(index + 1) * width, :] = ((old - scale * grad) * grow).astype(bf16)

    for index in (2, 0, 1):
        flips[:, index * width:(index + 1) * width] = news[index * width:(index + 1) * width, :].T

    def ahead(slot):
        low = slot * count
        all_q = q[0, :, :, low:low + count].reshape(wide, count)
        all_g = q[1, :, :, low:low + count].reshape(wide, count)
        both = jnp.dot(news[0:2 * width, :], all_q, preferred_element_type=f32)
        query_back = jnp.dot(news[2 * width:3 * width, :], all_g, preferred_element_type=f32)
        query_gate, query_up = both[0:width], both[width:2 * width]
        sigma = jax.nn.sigmoid(query_gate)
        silu = query_gate * sigma
        act = (silu * query_up).astype(bf16)
        grads = jnp.concatenate([
            (query_back * query_up * (sigma * (1.0 + query_gate * (1.0 - sigma)))).astype(bf16),
            (query_back * silu).astype(bf16),
        ], axis=0)
        return ((2 * width, act), (0, grads))

    def hand(slot, which, side_by):
        low, right = side_by
        value = jnp.dot(flips[:, low:low + right.shape[0]], right, preferred_element_type=f32)
        parts[slot, :, which] = value.reshape(2, half, count)
        give[slot, which] = parts[slot, 1 - core, which].astype(bf16)
        copy = remote(give.at[slot, which], got.at[slot, which], part_send.at[slot, which],
                      part_recv.at[slot, which], hid=1 - core)
        go(copy)
        return copy

    def cross(which, copy):
        copy.wait_recv()
        give[2, which] = (parts[1, core, which] + got[1, which].astype(f32)).astype(bf16)
        back = remote(give.at[2, which], got.at[2, which], part_send.at[2, which], part_recv.at[2, which], tok=side)
        go(back)
        return back

    away = [hand(1, which, entry) for which, entry in enumerate(ahead(1))]
    nearby = ahead(0)
    backs = [cross(which, copy) for which, copy in enumerate(away)]
    here = [hand(0, which, entry) for which, entry in enumerate(nearby)]
    for which in range(2):
        here[which].wait_recv()
        value = parts[0, core, which] + got[0, which].astype(f32)
        backs[which].wait_recv()
        result[which] = value + got[2, which].astype(f32)

    for copy in sends:
        copy.wait_send()
    for level in range(DEPTH):
        for m in range(3):
            @pl.when((z >= level) & (z < DEPTH - 1))
            def _():
                run(m, level, 0).wait_send()

            @pl.when((z <= level) & (z > 0))
            def _():
                run(m, level, 1).wait_send()

            @pl.when(z != level)
            def _():
                over(m, level).wait_send()

    @pl.when(is_end)
    def _():
        for index in range(pieces):
            to_end(index).wait_send()

    @pl.when(jnp.logical_not(is_end))
    def _():
        for index in range(1, 8):
            trade(index).wait_send()
        for index in range(pieces):
            to_mid(index).wait_send()
            to_fin(index).wait_send()


def shards_fast(
    tok, input_keys, input_values, input_lr, gate_weight, up_weight, down_weight, queries, out_grad
):
    rows, cols = gate_weight.shape
    width = cols // 2
    tokens, half = input_keys.shape
    count = queries.shape[0]
    wide = 2 * half
    pieces = 24
    size = width // pieces
    f32, bf16, dma = jnp.float32, jnp.bfloat16, pltpu.SemaphoreType.DMA
    flow = (pieces, 3, size, wide)
    result = pl.pallas_call(
        functools.partial(whole_kernel, tok, 2 * cols, pieces),
        out_shape=pltpu.VMEM((2, half, count), f32),
        in_specs=[HBM, HBM, HBM, HBM, HBM, HBM, HBM, HBM],
        out_specs=VM,
        scratch_shapes=[
            pltpu.VMEM((2, 2, half, 2 * tokens), bf16),
            pltpu.VMEM((half, tokens), bf16),
            pltpu.VMEM((1, tokens), f32),
            pltpu.VMEM((3 * rows, cols), bf16),
            pltpu.VMEM((tok, 3 * rows, width), bf16),
            pltpu.VMEM((3 * width, wide), bf16),
            pltpu.VMEM((3, 2, width // 3, 2 * tokens), bf16),
            pltpu.VMEM((width, 2 * tokens), bf16),
            pltpu.VMEM((3, 3, width // 3, wide), f32),
            pltpu.VMEM(flow, bf16),
            pltpu.VMEM(flow, bf16),
            pltpu.VMEM(flow, bf16),
            pltpu.VMEM(flow, bf16),
            pltpu.VMEM((4, 16, wide), f32),
            pltpu.VMEM((6, 8, wide), f32),
            pltpu.VMEM((3 * width, wide), bf16),
            pltpu.VMEM((wide, 3 * width), bf16),
            pltpu.VMEM((2, 2, half, 2 * count), bf16),
            pltpu.VMEM((2, 2, 2, half, count), f32),
            pltpu.VMEM((3, 2, half, count), bf16),
            pltpu.VMEM((3, 2, half, count), bf16),
            dma((8,)), dma((3,)), dma((3,)), dma((3, 2, DEPTH)), dma((3, DEPTH)), dma((3, DEPTH)), dma((3, DEPTH)),
            dma((4,)), dma((4,)), dma((5,)), dma((5,)), dma((2,)), dma((2,)),
            dma((pieces,)), dma((pieces,)), dma((pieces,)), dma((pieces,)), dma((pieces,)), dma((pieces,)),
            dma((8,)), dma((4,)), dma((3, 2)), dma((3, 2)),
        ],
        compiler_params=pltpu.CompilerParams(
            collective_id=0, has_side_effects=True, vmem_limit_bytes=60_000_000
        ),
    )(
        input_keys.T, input_values.T, input_lr.reshape(1, tokens), queries.T, out_grad.T,
        gate_weight, up_weight, down_weight,
    )
    return (result[0].astype(bf16).T, result[1].astype(bf16).T)


def fits(mesh, gate_weight, input_keys, queries):
    scene, tok, hid = (mesh.shape[name] for name in ("scene", "tok", "hid"))
    if (scene, tok, hid) != (2, WIDE * DEPTH, 2):
        return False
    depth, width = gate_weight.shape
    rows, half = depth // tok, input_keys.shape[1] // 2
    tokens, count = input_keys.shape[0] // (scene * tok), queries.shape[0] // (scene * tok)
    return (
        rows % 16 == 0 and half % 16 == 0 and 2 * half == depth
        and width % 1536 == 0 and tokens % 1024 == 0 and count % 128 == 0
    )


def solution(mesh):
    tok = mesh.shape["tok"]
    specs = (
        P(("scene", "tok"), "hid"),
        P(("scene", "tok"), "hid"),
        P(("scene", "tok")),
        P("tok", "hid"),
        P("tok", "hid"),
        P("tok", "hid"),
        P(("scene", "tok"), "hid"),
        P(("scene", "tok"), "hid"),
    )

    def run(*args):
        fast = fits(mesh, args[3], args[0], args[6])
        shards = functools.partial(shards_fast, tok) if fast else shards_plain
        return jax.shard_map(
            shards,
            mesh=mesh,
            in_specs=specs,
            out_specs=(P(("scene", "tok"), "hid"), P(("scene", "tok"), "hid")),
            check_vma=False,
        )(*args)

    return run
```

```python
import functools

import jax
import jax.numpy as jnp
from jax import lax
from jax.experimental import pallas as pl
from jax.experimental.pallas import tpu as pltpu
from jax.sharding import PartitionSpec as P

HID = 1536


step_ratio = 0.5
epsilon = 1e-06


def silu_slope(pre):
    sigma = jax.nn.sigmoid(pre)
    return sigma * (1.0 + pre * (1.0 - sigma))


def contract_rows(left, right):
    return lax.dot_general(
        left, right, (((0,), (0,)), ((), ())), preferred_element_type=jnp.float32
    )


def contract_cols(left, right):
    return lax.dot_general(
        left, right, (((1,), (1,)), ((), ())), preferred_element_type=jnp.float32
    )


def finish(moved, wsq, msq):
    return (moved * (jnp.sqrt(wsq) / jnp.sqrt(msq + epsilon))[:, None]).astype(jnp.bfloat16)


def shards_plain(
    input_keys, input_values, input_lr, gate_weight, up_weight, down_weight, queries, out_grad
):
    keys, values = (
        lax.all_gather(input_keys, "hid", axis=1, tiled=True),
        lax.all_gather(input_values, "hid", axis=1, tiled=True),
    )
    w_gate, w_up, w_down = (
        lax.all_gather(gate_weight, "tok", axis=0, tiled=True),
        lax.all_gather(up_weight, "tok", axis=0, tiled=True),
        lax.all_gather(down_weight, "tok", axis=0, tiled=True),
    )
    scaled = (input_lr[:, None] * values.astype(jnp.float32)).astype(jnp.bfloat16)
    key_gate = jnp.dot(keys, w_gate, preferred_element_type=jnp.float32)
    key_up = jnp.dot(keys, w_up, preferred_element_type=jnp.float32)
    gate_act = jax.nn.silu(key_gate)
    key_act = (gate_act * key_up).astype(jnp.bfloat16)
    back = jnp.dot(scaled, w_down, preferred_element_type=jnp.float32)
    d_gate = (-back * key_up * silu_slope(key_gate)).astype(jnp.bfloat16)
    d_up = (-back * gate_act).astype(jnp.bfloat16)
    width = gate_weight.shape[1]
    grads = lax.psum(
        jnp.concatenate(
            [
                contract_rows(keys, d_gate),
                contract_rows(keys, d_up),
                -contract_rows(scaled, key_act),
            ],
            axis=1,
        ),
        "tok",
    )
    olds = (w_gate, w_up, w_down)
    pieces = [grads[:, :width], grads[:, width : 2 * width], grads[:, 2 * width :]]
    weights = [old.astype(jnp.float32) for old in olds]
    renewed = []
    stats = []
    for weight, grad in zip(weights, pieces):
        stats.append(jnp.sum(weight * weight, axis=1))
        stats.append(jnp.sum(weight * grad, axis=1))
        stats.append(jnp.sum(grad * grad, axis=1))
    totals = lax.psum(
        (stats[0], stats[1], stats[2], stats[3], stats[4], stats[5], stats[6], stats[7], stats[8]),
        "hid",
    )
    for index in range(3):
        wsq = totals[3 * index] / HID
        cross = totals[3 * index + 1] / HID
        gsq = totals[3 * index + 2] / HID
        scale = step_ratio * jnp.sqrt(wsq) / jnp.sqrt(gsq + epsilon)
        moved = weights[index] - scale[:, None] * pieces[index]
        msq = wsq - 2.0 * scale * cross + scale * scale * gsq
        renewed.append(finish(moved, wsq, msq))
    new_gate, new_up, new_down = (renewed[0], renewed[1], renewed[2])
    query_rows, grad_rows = (
        lax.all_gather(queries, "hid", axis=1, tiled=True),
        lax.all_gather(out_grad, "hid", axis=1, tiled=True),
    )
    query_gate = jnp.dot(query_rows, new_gate, preferred_element_type=jnp.float32)
    query_up = jnp.dot(query_rows, new_up, preferred_element_type=jnp.float32)
    query_silu = jax.nn.silu(query_gate)
    query_act = (query_silu * query_up).astype(jnp.bfloat16)
    out_part = contract_cols(query_act, new_down)
    query_back = jnp.dot(grad_rows, new_down, preferred_element_type=jnp.float32)
    q_gate_grad = (query_back * query_up * silu_slope(query_gate)).astype(jnp.bfloat16)
    q_up_grad = (query_back * query_silu).astype(jnp.bfloat16)
    grad_part = contract_cols(q_gate_grad, new_gate) + contract_cols(q_up_grad, new_up)
    out_sum, grad_sum = (
        lax.psum_scatter(
            out_part.astype(jnp.bfloat16), "hid", scatter_dimension=1, tiled=True
        ).astype(jnp.float32),
        lax.psum_scatter(
            grad_part.astype(jnp.bfloat16), "hid", scatter_dimension=1, tiled=True
        ).astype(jnp.float32),
    )
    return (out_sum.astype(jnp.bfloat16), grad_sum.astype(jnp.bfloat16))


MESH = pl.DeviceIdType.MESH
WIDE = 2
DEPTH = 4
HBM = pl.BlockSpec(memory_space=pltpu.HBM)
VM = pl.BlockSpec(memory_space=pltpu.VMEM)


def remote(src, dst, send, recv, **where):
    return pltpu.make_async_remote_copy(
        src_ref=src, dst_ref=dst, send_sem=send, recv_sem=recv,
        device_id=where, device_id_type=MESH,
    )


def bend(level):
    return 0


def chip_of(level, color):
    return level * WIDE + lax.rem(color + bend(level), 2)


def whole_kernel(
    tok, hidden, pieces,
    keys_in, vals_in, lr_in, q_in, g_in, gate_in, up_in, down_in,
    result,
    toks, vraw, lr, own, olds, turned, d_pre, acts, acc, mine, from_end, from_mid, total,
    stats, squares, tallies, news, flips, q, parts, give, got,
    local, hop_send, hop_recv, run_send, run_recv, over_send, over_recv,
    tok_send, tok_recv, pass_send, pass_recv, ask_send, ask_recv,
    end_send, end_recv, mid_send, mid_recv, fin_send, fin_recv,
    stat_send, stat_recv, square_send, square_recv, part_send, part_recv,
):
    f32, bf16 = jnp.float32, jnp.bfloat16
    scene, core, rank = lax.axis_index("scene"), lax.axis_index("hid"), lax.axis_index("tok")
    z, x = lax.div(rank, WIDE), lax.rem(rank, WIDE)
    color = lax.rem(x + bend(z), 2)
    rows = gate_in.shape[0]
    half, tokens = keys_in.shape
    count = q_in.shape[1]
    width = olds.shape[2]
    wide = 2 * half
    near = z + 1 - 2 * lax.rem(z, 2)
    side = z * WIDE + 1 - x
    stack = near * WIDE + x
    is_end = (z == 0) | (z == DEPTH - 1)

    def same(level):
        return chip_of(level, color)

    barrier = pltpu.get_barrier_semaphore()
    peers = [{"hid": 1 - core}, {"scene": 1 - scene}, {"tok": side}, {"tok": side, "hid": 1 - core}]
    across = near * WIDE + 1 - x
    peers += [{"tok": same(near), "hid": 1 - core}, {"tok": across}, {"tok": across, "hid": 1 - core}]
    for where in peers:
        pl.semaphore_signal(barrier, inc=1, device_id=where, device_id_type=MESH)

    @pl.when(z > 0)
    def _():
        pl.semaphore_signal(barrier, inc=1, device_id={"tok": same(z - 1)}, device_id_type=MESH)

    @pl.when(z < DEPTH - 1)
    def _():
        pl.semaphore_signal(barrier, inc=1, device_id={"tok": same(z + 1)}, device_id_type=MESH)

    loads = []
    for index, (src, dst) in enumerate((
        (gate_in, own.at[0:rows]),
        (up_in, own.at[rows:2 * rows]),
        (down_in, own.at[2 * rows:3 * rows]),
        (vals_in, vraw),
        (lr_in, lr),
        (keys_in, toks.at[0, core, :, 0:tokens]),
        (q_in, q.at[0, core, :, 0:count]),
        (g_in, q.at[1, core, :, 0:count]),
    )):
        loads.append(pltpu.make_async_copy(src, dst, local.at[index]))
        loads[-1].start()
    for load in loads[:3]:
        load.wait()

    @pl.when(is_end)
    def _():
        pl.semaphore_wait(barrier, len(peers) + 1)

    @pl.when(jnp.logical_not(is_end))
    def _():
        pl.semaphore_wait(barrier, len(peers) + 2)

    sends = []

    def go(copy):
        copy.start()
        sends.append(copy)

    mycols = pl.ds(pl.multiple_of(color * width, width), width)
    sidecols = pl.ds(pl.multiple_of((1 - color) * width, width), width)
    strips = [slice(index * rows, (index + 1) * rows) for index in range(3)]
    leads = color == scene

    def hop(m):
        return remote(own.at[strips[m], sidecols], olds.at[rank, strips[m]], hop_send.at[m], hop_recv.at[m], tok=side)

    def run(m, level, way, src=None):
        dst = olds.at[chip_of(level, scene), strips[m]]
        target = z + 1 if way == 0 else z - 1
        return remote(dst if src is None else src, dst, run_send.at[m, way, level], run_recv.at[m, level],
                      tok=same(target))

    def over(m, level):
        block = olds.at[chip_of(level, scene), strips[m]]
        return remote(block, block, over_send.at[m, level], over_recv.at[m, level], scene=1 - scene)

    def launch(m, src):
        @pl.when(z < DEPTH - 1)
        def _():
            run(m, z, 0, src).start()

        @pl.when(z > 0)
        def _():
            run(m, z, 1, src).start()

    for m in range(3):
        go(hop(m))

        @pl.when(leads)
        def _():
            launch(m, own.at[strips[m], mycols])

    for load in loads[3:]:
        load.wait()
    toks[1, core, :, 0:tokens] = (lr[...] * vraw[...].astype(f32)).astype(bf16)
    swap = remote(toks.at[:, core, :, 0:tokens], toks.at[:, core, :, 0:tokens],
                  pass_send.at[0], pass_recv.at[0], hid=1 - core)
    go(swap)

    unit = tokens // 8
    spans = ((0, 3), (3, 2), (5, 2), (7, 1))
    inward = []
    for index, (low, size) in enumerate(spans):
        at = pl.ds(low * unit, size * unit)
        to = pl.ds(tokens + low * unit, size * unit)
        inward.append(remote(toks.at[:, core, :, at], toks.at[:, core, :, to],
                             tok_send.at[index], tok_recv.at[index], tok=side))
        go(inward[index])
    olds[rank] = own[:, mycols]

    @pl.when(jnp.logical_not(leads))
    def _():
        for m in range(3):
            block = olds.at[side, strips[m]]
            remote(block, block, hop_send.at[m], hop_recv.at[m], tok=side).wait_recv()
            launch(m, block)

    for step in range(1, DEPTH):
        for m in range(3):
            @pl.when(z >= step)
            def _():
                run(m, z - step, 0).wait_recv()

                @pl.when(z < DEPTH - 1)
                def _():
                    run(m, z - step, 0).start()
                over(m, z - step).start()

            @pl.when(z + step < DEPTH)
            def _():
                run(m, z + step, 1).wait_recv()

                @pl.when(z > 0)
                def _():
                    run(m, z + step, 1).start()
                over(m, z + step).start()

    @pl.when(leads)
    def _():
        for m in range(3):
            block = olds.at[side, strips[m]]
            remote(block, block, hop_send.at[m], hop_recv.at[m], tok=side).wait_recv()

    for step in range(1, DEPTH):
        for m in range(3):
            level = lax.rem(z + step, DEPTH)
            block = olds.at[chip_of(level, 1 - scene), strips[m]]
            remote(block, block, over_send.at[m, level], over_recv.at[m, level], scene=1 - scene).wait_recv()

    for index in range(3):
        block = olds[:, index * rows:(index + 1) * rows, :].reshape(wide, width)
        turned[index * width:(index + 1) * width, :] = block.T

    third = width // 3

    def forward(part, start, size):
        at = pl.ds(start, size)
        k = toks[0, :, :, at].reshape(wide, size)
        s = toks[1, :, :, at].reshape(wide, size)
        gate, up, down = (turned[m * width + part * third:m * width + (part + 1) * third, :] for m in range(3))
        both = jnp.dot(jnp.concatenate([gate, up], axis=0), k, preferred_element_type=f32)
        a, b = both[0:third], both[third:2 * third]
        back = -jnp.dot(down, s, preferred_element_type=f32)
        sigma = jax.nn.sigmoid(a)
        act = a * sigma
        acts[part * third:(part + 1) * third, at] = (act * b).astype(bf16)
        d_pre[part, 0, :, at] = (back * b * (sigma * (1.0 + a * (1.0 - sigma)))).astype(bf16)
        d_pre[part, 1, :, at] = (back * act).astype(bf16)

    relays = []

    def relay(index):
        inward[index].wait_recv()
        low, size = spans[index]
        block = toks.at[:, core, :, pl.ds(tokens + low * unit, size * unit)]
        copy = remote(block, block, pass_send.at[1 + index], pass_recv.at[1 + index], hid=1 - core)
        go(copy)
        relays.append(copy)

    def gradient(part, start, size, more):
        at = pl.ds(start, size)
        k = toks[0, :, :, at].reshape(wide, size)
        s = toks[1, :, :, at].reshape(wide, size)
        both = contract_cols(d_pre[part, :, :, at].reshape(2 * third, size), k).reshape(2, third, wide)
        down = -contract_cols(acts[part * third:(part + 1) * third, at], s)
        if more:
            both, down = acc[part, 0:2] + both, acc[part, 2] + down
        acc[part, 0:2] = both
        acc[part, 2] = down

    def span_of(index):
        low, size = spans[index]
        return tokens + low * unit, size * unit

    swap.wait_recv()
    half_tokens = tokens // 2
    forward(0, 0, half_tokens)
    relay(0)
    forward(0, half_tokens, half_tokens)
    relay(1)
    forward(1, 0, half_tokens)
    relays[0].wait_recv()
    forward(0, *span_of(0))
    relay(2)
    relays[1].wait_recv()
    forward(0, *span_of(1))
    cut = tokens + spans[2][0] * unit
    gradient(0, 0, cut, False)
    forward(1, half_tokens, half_tokens)
    forward(2, 0, half_tokens)
    relay(3)
    ask = remote(q.at[:, core, :, 0:count], q.at[:, core, :, count:2 * count],
                 ask_send.at[0], ask_recv.at[0], tok=side)
    go(ask)
    relays[2].wait_recv()
    forward(0, *span_of(2))
    forward(1, tokens, spans[3][0] * unit)
    relays[3].wait_recv()
    forward(0, *span_of(3))

    each = pieces // 3
    size = third // each

    def to_end(index):
        return remote(mine.at[index], from_end.at[index], end_send.at[index], end_recv.at[index], tok=same(near))

    def to_mid(index):
        return remote(mine.at[index], from_mid.at[index], mid_send.at[index], mid_recv.at[index],
                      tok=same(DEPTH - 1 - z))

    def to_fin(index):
        return remote(total.at[index], total.at[index], fin_send.at[index], fin_recv.at[index], tok=same(near))

    def local_piece(index):
        part, at = index // each, (index % each) * size
        return acc[part, :, at:at + size]

    for part in range(3):
        if part == 0:
            gradient(0, cut, 2 * tokens - cut, True)
        elif part == 1:
            forward(1, *span_of(3))
            gradient(1, 0, 2 * tokens, False)
        else:
            forward(2, half_tokens, half_tokens)
            forward(2, tokens, half_tokens)
            forward(2, tokens + half_tokens, half_tokens)
            gradient(2, 0, 2 * tokens, False)

        @pl.when(is_end)
        def _():
            for index in range(part * each, (part + 1) * each):
                mine[index] = local_piece(index).astype(bf16)
                to_end(index).start()

    ask.wait_recv()
    asked = q.at[:, core]
    ask_pass = remote(asked, asked, ask_send.at[1], ask_recv.at[1], hid=1 - core)
    go(ask_pass)

    lag = 4
    rowsum = lambda value: jnp.sum(value, axis=0, keepdims=True)

    def tally(index):
        for matrix in range(3):
            old = turned[matrix * width + index * size:matrix * width + (index + 1) * size, :].astype(f32)
            grad = total[index, matrix].astype(f32)
            tallies[2 * matrix] += jnp.sum((old * grad).reshape(size // 8, 8, wide), axis=0)
            tallies[2 * matrix + 1] += jnp.sum((grad * grad).reshape(size // 8, 8, wide), axis=0)

    def trade(index):
        dx, dc = (index // 2) % 2, index % 2
        level = z if index < 4 else near
        where = {"tok": level * WIDE + (1 - x if dx else x)}
        if dc:
            where["hid"] = 1 - core
        slot = 2 * dx + dc
        return remote(stats.at[0], stats.at[slot], stat_send.at[index], stat_recv.at[slot], **where)

    for index in range(3):
        old = turned[index * width:(index + 1) * width, :].astype(f32)
        squares[0, index:index + 1, :] = rowsum(old * old)
    swaps = []
    for index, where in enumerate(({"hid": 1 - core}, {"tok": side}, {"tok": side, "hid": 1 - core})):
        swaps.append(remote(squares.at[0], squares.at[index + 1], square_send.at[index], square_recv.at[index], **where))
        go(swaps[-1])

    @pl.when(jnp.logical_not(is_end))
    def _():
        tallies[...] = jnp.zeros_like(tallies)
        for turn in range(pieces + lag):
            if turn < pieces:
                to_end(turn).wait_recv()
                part, at = turn // each, (turn % each) * size
                summed = local_piece(turn) + from_end[turn].astype(f32)
                acc[part, :, at:at + size] = summed
                mine[turn] = summed.astype(bf16)
                to_mid(turn).start()
            if turn >= lag:
                index = turn - lag
                to_mid(index).wait_recv()
                total[index] = (local_piece(index) + from_mid[index].astype(f32)).astype(bf16)
                to_fin(index).start()
                tally(index)

        for index in range(3):
            for kind in range(2):
                at = 2 * index + kind
                stats[0, at:at + 1, :] = rowsum(tallies[2 * index + kind])
        for index in (7, 6, 5, 4, 3, 2, 1):
            trade(index).start()
        for index in (1, 2, 3):
            trade(index).wait_recv()

    @pl.when(is_end)
    def _():
        for index in range(pieces):
            to_fin(index).wait_recv()
        for index in range(4):
            trade(index).wait_recv()

    for copy in swaps:
        copy.wait_recv()
    ask_pass.wait_recv()
    table = (stats[0] + stats[1] + stats[2] + stats[3]) / hidden
    base = (squares[0] + squares[1] + squares[2] + squares[3]) / hidden
    for index in (2, 0, 1):
        wsq = base[index:index + 1, :]
        cross_sum, gsq = (table[2 * index + kind:2 * index + kind + 1, :] for kind in range(2))
        scale = step_ratio * jnp.sqrt(wsq) / jnp.sqrt(gsq + epsilon)
        msq = wsq - 2.0 * scale * cross_sum + scale * scale * gsq
        grow = jnp.sqrt(wsq) / jnp.sqrt(msq + epsilon)
        old = turned[index * width:(index + 1) * width, :].astype(f32)
        grad = total[:, index].reshape(width, wide).astype(f32)
        news[index * width:(index + 1) * width, :] = ((old - scale * grad) * grow).astype(bf16)

    for index in (2, 0, 1):
        flips[:, index * width:(index + 1) * width] = news[index * width:(index + 1) * width, :].T

    def ahead(slot):
        low = slot * count
        all_q = q[0, :, :, low:low + count].reshape(wide, count)
        all_g = q[1, :, :, low:low + count].reshape(wide, count)
        both = jnp.dot(news[0:2 * width, :], all_q, preferred_element_type=f32)
        query_back = jnp.dot(news[2 * width:3 * width, :], all_g, preferred_element_type=f32)
        query_gate, query_up = both[0:width], both[width:2 * width]
        sigma = jax.nn.sigmoid(query_gate)
        silu = query_gate * sigma
        act = (silu * query_up).astype(bf16)
        grads = jnp.concatenate([
            (query_back * query_up * (sigma * (1.0 + query_gate * (1.0 - sigma)))).astype(bf16),
            (query_back * silu).astype(bf16),
        ], axis=0)
        return ((2 * width, act), (0, grads))

    def hand(slot, which, side_by):
        low, right = side_by
        value = jnp.dot(flips[:, low:low + right.shape[0]], right, preferred_element_type=f32)
        parts[slot, :, which] = value.reshape(2, half, count)
        give[slot, which] = parts[slot, 1 - core, which].astype(bf16)
        copy = remote(give.at[slot, which], got.at[slot, which], part_send.at[slot, which],
                      part_recv.at[slot, which], hid=1 - core)
        go(copy)
        return copy

    def cross(which, copy):
        copy.wait_recv()
        give[2, which] = (parts[1, core, which] + got[1, which].astype(f32)).astype(bf16)
        back = remote(give.at[2, which], got.at[2, which], part_send.at[2, which], part_recv.at[2, which], tok=side)
        go(back)
        return back

    away = [hand(1, which, entry) for which, entry in enumerate(ahead(1))]
    backs = [cross(which, copy) for which, copy in enumerate(away)]
    nearby = ahead(0)
    here = [hand(0, which, entry) for which, entry in enumerate(nearby)]
    for which in range(2):
        here[which].wait_recv()
        value = parts[0, core, which] + got[0, which].astype(f32)
        backs[which].wait_recv()
        result[which] = value + got[2, which].astype(f32)

    for copy in sends:
        copy.wait_send()
    for level in range(DEPTH):
        for m in range(3):
            @pl.when((z >= level) & (z < DEPTH - 1))
            def _():
                run(m, level, 0).wait_send()

            @pl.when((z <= level) & (z > 0))
            def _():
                run(m, level, 1).wait_send()

            @pl.when(z != level)
            def _():
                over(m, level).wait_send()

    @pl.when(is_end)
    def _():
        for index in range(pieces):
            to_end(index).wait_send()

    @pl.when(jnp.logical_not(is_end))
    def _():
        for index in range(1, 8):
            trade(index).wait_send()
        for index in range(pieces):
            to_mid(index).wait_send()
            to_fin(index).wait_send()


def shards_fast(
    tok, input_keys, input_values, input_lr, gate_weight, up_weight, down_weight, queries, out_grad
):
    rows, cols = gate_weight.shape
    width = cols // 2
    tokens, half = input_keys.shape
    count = queries.shape[0]
    wide = 2 * half
    pieces = 24
    size = width // pieces
    f32, bf16, dma = jnp.float32, jnp.bfloat16, pltpu.SemaphoreType.DMA
    flow = (pieces, 3, size, wide)
    result = pl.pallas_call(
        functools.partial(whole_kernel, tok, 2 * cols, pieces),
        out_shape=pltpu.VMEM((2, half, count), f32),
        in_specs=[HBM, HBM, HBM, HBM, HBM, HBM, HBM, HBM],
        out_specs=VM,
        scratch_shapes=[
            pltpu.VMEM((2, 2, half, 2 * tokens), bf16),
            pltpu.VMEM((half, tokens), bf16),
            pltpu.VMEM((1, tokens), f32),
            pltpu.VMEM((3 * rows, cols), bf16),
            pltpu.VMEM((tok, 3 * rows, width), bf16),
            pltpu.VMEM((3 * width, wide), bf16),
            pltpu.VMEM((3, 2, width // 3, 2 * tokens), bf16),
            pltpu.VMEM((width, 2 * tokens), bf16),
            pltpu.VMEM((3, 3, width // 3, wide), f32),
            pltpu.VMEM(flow, bf16),
            pltpu.VMEM(flow, bf16),
            pltpu.VMEM(flow, bf16),
            pltpu.VMEM(flow, bf16),
            pltpu.VMEM((4, 8, wide), f32),
            pltpu.VMEM((4, 8, wide), f32),
            pltpu.VMEM((6, 8, wide), f32),
            pltpu.VMEM((3 * width, wide), bf16),
            pltpu.VMEM((wide, 3 * width), bf16),
            pltpu.VMEM((2, 2, half, 2 * count), bf16),
            pltpu.VMEM((2, 2, 2, half, count), f32),
            pltpu.VMEM((3, 2, half, count), bf16),
            pltpu.VMEM((3, 2, half, count), bf16),
            dma((8,)), dma((3,)), dma((3,)), dma((3, 2, DEPTH)), dma((3, DEPTH)), dma((3, DEPTH)), dma((3, DEPTH)),
            dma((4,)), dma((4,)), dma((5,)), dma((5,)), dma((2,)), dma((2,)),
            dma((pieces,)), dma((pieces,)), dma((pieces,)), dma((pieces,)), dma((pieces,)), dma((pieces,)),
            dma((8,)), dma((4,)), dma((3,)), dma((3,)), dma((3, 2)), dma((3, 2)),
        ],
        compiler_params=pltpu.CompilerParams(
            collective_id=0, has_side_effects=True, vmem_limit_bytes=60_000_000
        ),
    )(
        input_keys.T, input_values.T, input_lr.reshape(1, tokens), queries.T, out_grad.T,
        gate_weight, up_weight, down_weight,
    )
    return (result[0].astype(bf16).T, result[1].astype(bf16).T)


def fits(mesh, gate_weight, input_keys, queries):
    scene, tok, hid = (mesh.shape[name] for name in ("scene", "tok", "hid"))
    if (scene, tok, hid) != (2, WIDE * DEPTH, 2):
        return False
    depth, width = gate_weight.shape
    rows, half = depth // tok, input_keys.shape[1] // 2
    tokens, count = input_keys.shape[0] // (scene * tok), queries.shape[0] // (scene * tok)
    return (
        rows % 16 == 0 and half % 16 == 0 and 2 * half == depth
        and width % 1536 == 0 and tokens % 1024 == 0 and count % 128 == 0
    )


def solution(mesh):
    tok = mesh.shape["tok"]
    specs = (
        P(("scene", "tok"), "hid"),
        P(("scene", "tok"), "hid"),
        P(("scene", "tok")),
        P("tok", "hid"),
        P("tok", "hid"),
        P("tok", "hid"),
        P(("scene", "tok"), "hid"),
        P(("scene", "tok"), "hid"),
    )

    def run(*args):
        fast = fits(mesh, args[3], args[0], args[6])
        shards = functools.partial(shards_fast, tok) if fast else shards_plain
        return jax.shard_map(
            shards,
            mesh=mesh,
            in_specs=specs,
            out_specs=(P(("scene", "tok"), "hid"), P(("scene", "tok"), "hid")),
            check_vma=False,
        )(*args)

    return run
```
